32 devices in a mesh: shot: 16 (over z, y, core), rcv: 2 (over x).
Axes of the slice: x: 2, y: 2, z: 4, core: 2. Of those that a mesh axis runs over, the one named last changes fastest.
Arguments:
- record: bfloat16 [768, 131072], P('rcv', 'shot'), may hold values from -6 to 6
- shot_fire_samples: int32 [512], P('shot'), may hold values from 0 to 131071, as said below
Outputs:
- psf_gram: float32 [2, 4, 768, 768], P(None, None, 'rcv', 'shot')
The draws below stay inside these ranges and needn't reach their ends.
Inputs may be any that keep to these rules, and one draw needn't show every extreme that they name: `shot_fire_samples`: shot s fires at a sample from s * 256 to s * 256 + 255.
All inputs are finite; a program needn't handle non-finite values.
Results may differ from the reference program's by a relative error of at most 0.0025.
Values may be sent and summed in bfloat16 or wider, within the bound.
A program may use at most 64 MiB of HBM per device.

```python
import math
import jax
import jax.numpy as jnp
from jax import lax

R = 768
WIN = 2048
F = 4
SPACING = 256
SHOTS_PER_UNIT = 32
SHOTS = 512
NT = 131072
N_SHOT = 16


def draw_shot_fire_samples(key, part):
    jitter = jax.random.randint(jax.random.fold_in(key, 7), (SHOTS,), 0, SPACING)
    return (jnp.arange(SHOTS, dtype=jnp.int32) * SPACING + jitter).astype(jnp.int32)


def shard_levels(key, shape, split, least, top_value):
    level, own = 1.0, jax.random.fold_in(key, 6)
    for dim, blocks in split:
        steps = jnp.exp(jax.random.uniform(jax.random.fold_in(own, dim), (blocks,), jnp.float32, least / len(split), top_value / len(split)))
        level = level * jnp.repeat(steps, shape[dim] // blocks).reshape([-1 if axis == dim else 1 for axis in range(len(shape))])
    return level


def normal_values(stream_key, shape, deviation, limit, split=(), kind=jnp.bfloat16):
    drawn = jax.random.normal(stream_key, shape, jnp.float32) * deviation
    if len(split) > 0:
        drawn = shard_levels(stream_key, shape, split, -0.22, 0.18) * drawn
    return jnp.clip(drawn, min=-limit, max=limit).astype(kind)


def setup_inputs(seed: int = 0) -> dict:
    arg_keys = jax.random.split(jax.random.key(seed), 3)
    record = normal_values(arg_keys[0], (R, NT), 1.0, 6.0, ((0, 2), (1, 16)))
    shot_fire_samples = draw_shot_fire_samples(jax.random.fold_in(arg_keys[2], 71), 0)
    return {"record": record, "shot_fire_samples": shot_fire_samples}


freq_bins = (24, 40, 56, 80)

def dft_table(window_len):
    lag_index = jnp.arange(window_len, dtype=jnp.int32)
    bin_list = jnp.array(freq_bins, dtype=jnp.int32)
    turn_count = lag_index[:, None] * bin_list[None, :] % window_len
    phase_angle = 2.0 * math.pi / window_len * turn_count.astype(jnp.float32)
    dft_rows = jnp.concatenate([jnp.cos(phase_angle), -jnp.sin(phase_angle)], axis=1) / math.sqrt(window_len)
    return dft_rows.astype(jnp.bfloat16)

def gram_terms(left, right):
    nfreq = len(freq_bins)
    left_re = left[:, :nfreq, :].astype(jnp.float32)
    left_im = left[:, nfreq:, :].astype(jnp.float32)
    right_re = right[:, :nfreq, :].astype(jnp.float32)
    right_im = right[:, nfreq:, :].astype(jnp.float32)
    gram_real = jnp.einsum('sfr,sfq->frq', left_re, right_re) + jnp.einsum('sfr,sfq->frq', left_im, right_im)
    gram_imag = jnp.einsum('sfr,sfq->frq', left_re, right_im) - jnp.einsum('sfr,sfq->frq', left_im, right_re)
    return jnp.stack([gram_real, gram_imag], axis=0)

def reference(record, shot_fire_samples):
    padded = jnp.concatenate([record, jnp.zeros((R, WIN), record.dtype)], axis=1)
    dft_rows = dft_table(WIN)

    def spectra_block(block_times):

        def cut_window(begin_at):
            return lax.dynamic_slice_in_dim(padded, begin_at.astype(jnp.int32), WIN, 1)
        windows = jax.vmap(cut_window)(block_times)
        flat = jnp.dot(windows.reshape(-1, WIN), dft_rows, preferred_element_type=jnp.float32)
        return flat.reshape(SHOTS_PER_UNIT, R, 2 * F).transpose(0, 2, 1).astype(jnp.bfloat16)
    trace_spectra = lax.map(spectra_block, shot_fire_samples.reshape(N_SHOT, SHOTS_PER_UNIT))
    trace_spectra = trace_spectra.reshape(SHOTS, 2 * F, R)
    return gram_terms(trace_spectra, trace_spectra) / SHOTS
```

```python
import functools
import math

import jax
import jax.numpy as jnp
from jax import lax
from jax.experimental import pallas as pl
from jax.experimental.pallas import tpu as pltpu
from jax.sharding import PartitionSpec as P

WIN = 2048
SPACING = 256


freq_bins = (24, 40, 56, 80)


def shifted(block, axis, distance):
    devices = range(lax.axis_size(axis))
    route = [(i - distance, i) for i in devices if i - distance in devices]
    return lax.ppermute(block, axis, route)


def dft_table(window_len):
    lag_index = jnp.arange(window_len, dtype=jnp.int32)
    bin_list = jnp.array(freq_bins, dtype=jnp.int32)
    turn_count = lag_index[:, None] * bin_list[None, :] % window_len
    phase_angle = 2.0 * math.pi / window_len * turn_count.astype(jnp.float32)
    dft_rows = jnp.concatenate([jnp.cos(phase_angle), -jnp.sin(phase_angle)], axis=1) / math.sqrt(
        window_len
    )
    return dft_rows.astype(jnp.bfloat16)


def shifted_tables(jitter, span):
    lag_index = jnp.arange(span, dtype=jnp.int32)[None, :] - jitter[:, None]
    inside = (lag_index >= 0) & (lag_index < WIN)
    clipped = jnp.clip(lag_index, 0, WIN - 1)
    bin_list = jnp.array(freq_bins, dtype=jnp.int32)
    turn_count = clipped[:, None, :] * bin_list[None, :, None] % WIN
    phase_angle = 2.0 * math.pi / WIN * turn_count.astype(jnp.float32)
    table = jnp.concatenate([jnp.cos(phase_angle), -jnp.sin(phase_angle)], axis=1) / math.sqrt(WIN)
    table = jnp.where(inside[:, None, :], table, 0.0)
    return table.astype(jnp.bfloat16)


def local_spectra(extended, sample_offsets, dft_rows):
    count_of_shots = sample_offsets.shape[0]
    reach_blocks = WIN // SPACING + 1
    jitter = sample_offsets - jnp.arange(count_of_shots, dtype=jnp.int32) * SPACING
    tables = shifted_tables(jitter, reach_blocks * SPACING)
    tables = tables.reshape(count_of_shots, dft_rows.shape[1], reach_blocks, SPACING)
    blocks = extended.reshape(extended.shape[0], extended.shape[1] // SPACING, SPACING)
    total = jnp.zeros((count_of_shots, dft_rows.shape[1], extended.shape[0]), jnp.float32)
    for offset in range(reach_blocks):
        record_part = blocks[:, offset : offset + count_of_shots, :]
        total = total + jnp.einsum(
            "rsu,scu->scr", record_part, tables[:, :, offset, :], preferred_element_type=jnp.float32
        )
    return total


def gram_terms(left, right):
    nfreq = len(freq_bins)
    left_re = left[:, :nfreq, :]
    left_im = left[:, nfreq:, :]
    right_re = right[:, :nfreq, :]
    right_im = right[:, nfreq:, :]
    gram_real = jnp.einsum("sfr,sfq->frq", left_re, right_re, preferred_element_type=jnp.float32)
    gram_real = gram_real + jnp.einsum(
        "sfr,sfq->frq", left_im, right_im, preferred_element_type=jnp.float32
    )
    gram_imag = jnp.einsum("sfr,sfq->frq", left_re, right_im, preferred_element_type=jnp.float32)
    gram_imag = gram_imag - jnp.einsum(
        "sfr,sfq->frq", left_im, right_re, preferred_element_type=jnp.float32
    )
    return jnp.stack([gram_real, gram_imag], axis=0)


def per_device(record, shot_fire_samples):
    trace_segment_length = record.shape[1]
    count_of_shots = shot_fire_samples.shape[0]
    dft_rows = dft_table(WIN)
    sample_offsets = shot_fire_samples - lax.axis_index("shot") * trace_segment_length
    head_rows = record[:, :WIN]
    rim_rows = shifted(head_rows, "shot", -1)
    extended = jnp.concatenate([record, rim_rows], axis=1)
    trace_spectra = local_spectra(extended, sample_offsets, dft_rows)
    trace_spectra = trace_spectra.astype(jnp.bfloat16)
    all_receivers = lax.all_gather(trace_spectra, "rcv", axis=2, tiled=True)
    total_shots = count_of_shots * lax.axis_size("shot")
    row_side = lax.all_gather(trace_spectra, "shot", axis=0, tiled=True)
    column_side = lax.all_to_all(all_receivers, "shot", split_axis=2, concat_axis=0, tiled=True)
    result = gram_terms(row_side, column_side)
    return result / total_shots


LANES = 128
HALF = 16
GROUP = 8
SLOT = 64
MESH = pl.DeviceIdType.MESH


def lane_fields(shape):
    lane = lax.broadcasted_iota(jnp.int32, shape, len(shape) - 1)
    return lane // 32 % 4, lane // 16 % 2, lane % 16


def rotated(lag, off_row):
    freq, part, _ = lane_fields(lag.shape)
    bins = jnp.full(lag.shape, freq_bins[0], jnp.int32)
    for f in range(1, len(freq_bins)):
        bins = jnp.where(freq == f, freq_bins[f], bins)
    turn = ((lag & (SPACING - 1)) * bins + part * (WIN // 4)) & (WIN - 1)
    phase = (2.0 * math.pi / WIN) * turn.astype(jnp.float32)
    return jnp.cos(phase) / math.sqrt(WIN)


def kernel(
    n, off_ref, rec_ref, out_ref,
    rec, poff, table, tmask, rim_out, rim_in, gat, col, rmat, acc,
    rec_sem, jit_sem, rim_sem, ring_send, pair_send, chunk_recv, col_send, col_recv,
):
    me = lax.axis_index("shot")
    mj = lax.axis_index("rcv")
    rows = rec.shape[0]
    groups = rec.shape[1] // (GROUP * SPACING)
    span = GROUP * SPACING
    chips = n // 2
    nz = chips // 2
    ncol = col.shape[2]
    core = me % 2
    chip = me // 2
    z, y = chip // 2, chip % 2
    pos = jnp.where(y == 0, z, chips - 1 - z)

    def device_at(position, which):
        q = (position + 2 * chips) % chips
        second = q >= nz
        zz = jnp.where(second, chips - 1 - q, q)
        yy = jnp.where(second, 1, 0)
        return (zz * 2 + yy) * 2 + which

    cw, ccw = device_at(pos + 1, core), device_at(pos - 1, core)
    pair = chip * 2 + (1 - core)
    prev, nxt = (me + n - 1) % n, (me + 1) % n

    def load(g):
        part = pl.ds(g * span, span)
        return pltpu.make_async_copy(rec_ref.at[:, part], rec.at[:, part], rec_sem.at[g])

    for g in range(groups):
        load(g).start()

    barrier = pltpu.get_barrier_semaphore()
    for other in (cw, ccw, pair, prev, nxt):
        pl.semaphore_signal(barrier, inc=1, device_id=(other, mj), device_id_type=MESH)
    pl.semaphore_signal(barrier, inc=1, device_id=(me, 1 - mj), device_id_type=MESH)
    pl.semaphore_wait(barrier, 6)

    jitter = pltpu.make_async_remote_copy(
        off_ref, poff, jit_sem.at[0], jit_sem.at[1], device_id=(nxt, mj), device_id_type=MESH
    )
    jitter.start()

    def lag_of(off_row):
        u = lax.broadcasted_iota(jnp.int32, (SPACING, LANES), 0)
        return u - off_row

    def partial_spectra(off_row, groups_of):
        lag = lag_of(off_row)
        table[...] = rotated(lag, off_row)
        total = jnp.zeros((rows, LANES), jnp.float32)
        for g in groups_of:
            for b in range(GROUP):
                here = lag_of(off_row) + (g * GROUP + b) * SPACING
                inside = (here >= 0) & (here < WIN)
                tmask[pl.ds(b * SPACING, SPACING), :] = jnp.where(inside, table[...], 0.0).astype(
                    jnp.bfloat16
                )
            total = total + jnp.dot(
                rec[:, g * span : (g + 1) * span], tmask[...], preferred_element_type=jnp.float32
            )
        return total

    def ring(src, h, d):
        return pltpu.make_async_remote_copy(
            gat.at[src, h], gat.at[src, h], ring_send.at[d, src, h], chunk_recv.at[src, h],
            device_id=(cw if d == 0 else ccw, mj), device_id_type=MESH,
        )

    def share(src, h):
        return pltpu.make_async_remote_copy(
            gat.at[src, h], gat.at[src, h], pair_send.at[src, h], chunk_recv.at[src, h],
            device_id=(pair, mj), device_id_type=MESH,
        )

    home = me * ncol // rows
    provider = home == mj
    first = pl.multiple_of(jnp.where(provider, me * ncol - home * rows, 0), 16)

    def col_far(src, h):
        return pltpu.make_async_remote_copy(
            gat.at[src, h, pl.ds(first, ncol), :], col.at[src, h], col_send.at[src, h],
            col_recv.at[src, h], device_id=(me, 1 - mj), device_id_type=MESH,
        )

    def col_near(src, h):
        return pltpu.make_async_copy(
            gat.at[src, h, pl.ds(first, ncol), :], col.at[src, h], col_recv.at[src, h]
        )

    def send_col(src, h):
        @pl.when(provider)
        def _():
            col_far(src, h).start()
            col_near(src, h).start()

    def send_own(h):
        ring(me, h, 0).start()
        ring(me, h, 1).start()
        share(me, h).start()
        send_col(me, h)

    def gram(src):
        for h in range(2):
            x = col[src, h].astype(jnp.float32)
            freq, part, _ = lane_fields(x.shape)
            swapped = jnp.where(part == 0, pltpu.roll(x, LANES - 16, 1), -pltpu.roll(x, 16, 1))
            for ri, value in enumerate((x, swapped)):
                for f in range(4):
                    rmat[pl.ds((ri * 4 + f) * SLOT, ncol), h * LANES : (h + 1) * LANES] = jnp.where(
                        freq == f, value, 0.0
                    ).astype(jnp.bfloat16)
        left = jnp.concatenate([gat[src, 0], gat[src, 1]], axis=1)
        acc[...] += lax.dot_general(
            left, rmat[...], (((1,), (1,)), ((), ())), preferred_element_type=jnp.float32
        )

    off0 = off_ref[0:1, 0:LANES]
    off1 = off_ref[0:1, LANES : 2 * LANES]
    rmat[...] = jnp.zeros_like(rmat)
    acc[...] = jnp.zeros_like(acc)
    for g in range(groups):
        load(g).wait()
    gat[me, 0] = partial_spectra(off0, (0, 1, 2)).astype(jnp.bfloat16)
    send_own(0)

    jitter.wait()
    offp = poff[0:1, LANES : 2 * LANES] - rec.shape[1]
    foreign = partial_spectra(offp, (0,))
    cut = rows // 2
    rim_out[...] = foreign[:cut] + pltpu.roll(foreign[cut:], LANES - 8, 1)
    rim = pltpu.make_async_remote_copy(
        rim_out, rim_in, rim_sem.at[0], rim_sem.at[1], device_id=(prev, mj), device_id_type=MESH
    )
    rim.start()
    second = partial_spectra(off1, (2, 3))
    rim.wait()
    _, _, shot = lane_fields((cut, LANES))
    wanted = (shot >= 8) & (me < n - 1)
    upper = jnp.where(wanted, rim_in[...], 0.0)
    lower = jnp.where(wanted, pltpu.roll(rim_in[...], 8, 1), 0.0)
    gat[me, 1, :cut] = (second[:cut] + upper).astype(jnp.bfloat16)
    gat[me, 1, cut:] = (second[cut:] + lower).astype(jnp.bfloat16)
    send_own(1)

    half = chips // 2

    def hops(h, d):
        return half if h == d else half - 1

    def arrivals(t):
        found = []
        for h in range(2):
            for d in range(2):
                if 1 <= t <= hops(h, d):
                    found.append((h, d))
        return found

    def source(t, d, which):
        return device_at(pos - t if d == 0 else pos + t, which)

    def step_sources(t):
        if t == 0:
            return [0]
        return [0, 1] if t < half else [0]

    for t in range(half + 1):
        for h, d in arrivals(t):
            src = source(t, d, core)
            ring(src, h, d).wait_recv()
            if t < hops(h, d):
                ring(src, h, d).start()
            share(src, h).start()
            send_col(src, h)
        for d in step_sources(t):
            for h in range(2):
                src = source(t, d, 1 - core)
                share(src, h).wait_recv()
                send_col(src, h)
        for back in ((t - 1,) if t < half else (t - 1, t)):
            if back < 0:
                continue
            for d in step_sources(back):
                for which in range(2):
                    src = source(back, d, which)
                    for h in range(2):
                        col_near(src, h).wait()
                    gram(src)

    scale = 1.0 / (n * 2 * HALF)
    for g in range(8):
        out_ref[g // 4, g % 4] = acc[:, g * SLOT : g * SLOT + ncol] * scale

    for h in range(2):
        ring(me, h, 0).wait_send()
        ring(me, h, 1).wait_send()
    for t in range(1, half + 1):
        for h, d in arrivals(t):
            src = source(t, d, core)
            if t < hops(h, d):
                ring(src, h, d).wait_send()
            share(src, h).wait_send()
    for h in range(2):
        share(me, h).wait_send()

    @pl.when(provider)
    def _():
        for src in range(n):
            for h in range(2):
                col_far(src, h).wait_send()


def fused_device(n, ncol, record, shot_fire_samples):
    rows, length = record.shape
    off = shot_fire_samples - lax.axis_index("shot") * length
    off = jnp.broadcast_to(off.reshape(1, 2, 1, HALF), (8, 2, 8, HALF)).reshape(8, 2 * LANES)
    return pl.pallas_call(
        functools.partial(kernel, n),
        out_shape=jax.ShapeDtypeStruct((2, 4, rows, ncol), jnp.float32),
        in_specs=[
            pl.BlockSpec(memory_space=pltpu.VMEM),
            pl.BlockSpec(memory_space=pl.ANY),
        ],
        out_specs=pl.BlockSpec(memory_space=pltpu.VMEM),
        scratch_shapes=[
            pltpu.VMEM((rows, length), jnp.bfloat16),
            pltpu.VMEM((8, 2 * LANES), jnp.int32),
            pltpu.VMEM((SPACING, LANES), jnp.float32),
            pltpu.VMEM((GROUP * SPACING, LANES), jnp.bfloat16),
            pltpu.VMEM((rows // 2, LANES), jnp.float32),
            pltpu.VMEM((rows // 2, LANES), jnp.float32),
            pltpu.VMEM((n, 2, rows, LANES), jnp.bfloat16),
            pltpu.VMEM((n, 2, ncol, LANES), jnp.bfloat16),
            pltpu.VMEM((8 * SLOT, 2 * LANES), jnp.bfloat16),
            pltpu.VMEM((rows, 8 * SLOT), jnp.float32),
            pltpu.SemaphoreType.DMA((length // (GROUP * SPACING),)),
            pltpu.SemaphoreType.DMA((2,)),
            pltpu.SemaphoreType.DMA((2,)),
            pltpu.SemaphoreType.DMA((2, n, 2)),
            pltpu.SemaphoreType.DMA((n, 2)),
            pltpu.SemaphoreType.DMA((n, 2)),
            pltpu.SemaphoreType.DMA((n, 2)),
            pltpu.SemaphoreType.DMA((n, 2)),
        ],
        compiler_params=pltpu.CompilerParams(
            collective_id=0, has_side_effects=True, vmem_limit_bytes=40 * 1024 * 1024
        ),
    )(off, record)


def whole_step(n, receivers, record, shot_fire_samples):
    rows, length = record.shape
    shots = shot_fire_samples.shape[0]
    ncol = receivers // n
    fits = (
        receivers == 2 * rows and ncol % 16 == 0 and ncol <= SLOT and rows % (2 * ncol) == 0
        and shots == 2 * HALF and length == shots * SPACING and n % 8 == 0
    )
    if fits:
        return fused_device(n, ncol, record, shot_fire_samples)
    return per_device(record, shot_fire_samples)


def solution(mesh):
    def step(record, shot_fire_samples):
        body = functools.partial(whole_step, mesh.shape["shot"], record.shape[0])
        return jax.shard_map(
            body,
            mesh=mesh,
            in_specs=(P("rcv", "shot"), P("shot")),
            out_specs=P(None, None, "rcv", "shot"),
            check_vma=False,
        )(record, shot_fire_samples)

    return step
```

```python
import functools
import math

import jax
import jax.numpy as jnp
from jax import lax
from jax.experimental import pallas as pl
from jax.experimental.pallas import tpu as pltpu
from jax.sharding import PartitionSpec as P

WIN = 2048
SPACING = 256


freq_bins = (24, 40, 56, 80)


def shifted(block, axis, distance):
    devices = range(lax.axis_size(axis))
    route = [(i - distance, i) for i in devices if i - distance in devices]
    return lax.ppermute(block, axis, route)


def dft_table(window_len):
    lag_index = jnp.arange(window_len, dtype=jnp.int32)
    bin_list = jnp.array(freq_bins, dtype=jnp.int32)
    turn_count = lag_index[:, None] * bin_list[None, :] % window_len
    phase_angle = 2.0 * math.pi / window_len * turn_count.astype(jnp.float32)
    dft_rows = jnp.concatenate([jnp.cos(phase_angle), -jnp.sin(phase_angle)], axis=1) / math.sqrt(
        window_len
    )
    return dft_rows.astype(jnp.bfloat16)


def shifted_tables(jitter, span):
    lag_index = jnp.arange(span, dtype=jnp.int32)[None, :] - jitter[:, None]
    inside = (lag_index >= 0) & (lag_index < WIN)
    clipped = jnp.clip(lag_index, 0, WIN - 1)
    bin_list = jnp.array(freq_bins, dtype=jnp.int32)
    turn_count = clipped[:, None, :] * bin_list[None, :, None] % WIN
    phase_angle = 2.0 * math.pi / WIN * turn_count.astype(jnp.float32)
    table = jnp.concatenate([jnp.cos(phase_angle), -jnp.sin(phase_angle)], axis=1) / math.sqrt(WIN)
    table = jnp.where(inside[:, None, :], table, 0.0)
    return table.astype(jnp.bfloat16)


def local_spectra(extended, sample_offsets, dft_rows):
    count_of_shots = sample_offsets.shape[0]
    reach_blocks = WIN // SPACING + 1
    jitter = sample_offsets - jnp.arange(count_of_shots, dtype=jnp.int32) * SPACING
    tables = shifted_tables(jitter, reach_blocks * SPACING)
    tables = tables.reshape(count_of_shots, dft_rows.shape[1], reach_blocks, SPACING)
    blocks = extended.reshape(extended.shape[0], extended.shape[1] // SPACING, SPACING)
    total = jnp.zeros((count_of_shots, dft_rows.shape[1], extended.shape[0]), jnp.float32)
    for offset in range(reach_blocks):
        record_part = blocks[:, offset : offset + count_of_shots, :]
        total = total + jnp.einsum(
            "rsu,scu->scr", record_part, tables[:, :, offset, :], preferred_element_type=jnp.float32
        )
    return total


def gram_terms(left, right):
    nfreq = len(freq_bins)
    left_re = left[:, :nfreq, :]
    left_im = left[:, nfreq:, :]
    right_re = right[:, :nfreq, :]
    right_im = right[:, nfreq:, :]
    gram_real = jnp.einsum("sfr,sfq->frq", left_re, right_re, preferred_element_type=jnp.float32)
    gram_real = gram_real + jnp.einsum(
        "sfr,sfq->frq", left_im, right_im, preferred_element_type=jnp.float32
    )
    gram_imag = jnp.einsum("sfr,sfq->frq", left_re, right_im, preferred_element_type=jnp.float32)
    gram_imag = gram_imag - jnp.einsum(
        "sfr,sfq->frq", left_im, right_re, preferred_element_type=jnp.float32
    )
    return jnp.stack([gram_real, gram_imag], axis=0)


def per_device(record, shot_fire_samples):
    trace_segment_length = record.shape[1]
    count_of_shots = shot_fire_samples.shape[0]
    dft_rows = dft_table(WIN)
    sample_offsets = shot_fire_samples - lax.axis_index("shot") * trace_segment_length
    head_rows = record[:, :WIN]
    rim_rows = shifted(head_rows, "shot", -1)
    extended = jnp.concatenate([record, rim_rows], axis=1)
    trace_spectra = local_spectra(extended, sample_offsets, dft_rows)
    trace_spectra = trace_spectra.astype(jnp.bfloat16)
    all_receivers = lax.all_gather(trace_spectra, "rcv", axis=2, tiled=True)
    total_shots = count_of_shots * lax.axis_size("shot")
    row_side = lax.all_gather(trace_spectra, "shot", axis=0, tiled=True)
    column_side = lax.all_to_all(all_receivers, "shot", split_axis=2, concat_axis=0, tiled=True)
    result = gram_terms(row_side, column_side)
    return result / total_shots


LANES = 128
HALF = 16
GROUP = 8
MESH = pl.DeviceIdType.MESH


def lane_fields(shape):
    lane = lax.broadcasted_iota(jnp.int32, shape, len(shape) - 1)
    return lane // 32 % 4, lane // 16 % 2, lane % 16


def rotated(lag, off_row):
    freq, part, _ = lane_fields(lag.shape)
    bins = jnp.full(lag.shape, freq_bins[0], jnp.int32)
    for f in range(1, len(freq_bins)):
        bins = jnp.where(freq == f, freq_bins[f], bins)
    turn = ((lag & (SPACING - 1)) * bins + part * (WIN // 4)) & (WIN - 1)
    phase = (2.0 * math.pi / WIN) * turn.astype(jnp.float32)
    return jnp.cos(phase) / math.sqrt(WIN)


def kernel(
    n, fire_ref, rec_ref, out_ref,
    rec, joff, poff, table, tmask, rim_out, rim_in, gat, col, rmat, acc,
    rec_sem, jit_sem, rim_sem, ring_send, pair_send, chunk_recv, col_send, col_recv,
):
    me = lax.axis_index("shot")
    mj = lax.axis_index("rcv")
    rows = rec.shape[0]
    groups = rec.shape[1] // (GROUP * SPACING)
    span = GROUP * SPACING
    chips = n // 2
    nz = chips // 2
    ncol = col.shape[2]
    core = me % 2
    chip = me // 2
    z, y = chip // 2, chip % 2
    pos = jnp.where(y == 0, z, chips - 1 - z)

    def device_at(position, which):
        q = (position + 2 * chips) % chips
        second = q >= nz
        zz = jnp.where(second, chips - 1 - q, q)
        yy = jnp.where(second, 1, 0)
        return (zz * 2 + yy) * 2 + which

    cw, ccw = device_at(pos + 1, core), device_at(pos - 1, core)
    pair = chip * 2 + (1 - core)
    prev, nxt = (me + n - 1) % n, (me + 1) % n

    def load(g):
        part = pl.ds(g * span, span)
        return pltpu.make_async_copy(rec_ref.at[:, part], rec.at[:, part], rec_sem.at[g])

    for g in range(groups):
        load(g).start()

    _, _, shot_lane = lane_fields((1, LANES))
    offs = []
    for h in range(2):
        row = jnp.zeros((1, LANES), jnp.int32)
        for s in range(HALF):
            row = jnp.where(shot_lane == s, fire_ref[h * HALF + s], row)
        offs.append(row - me * rec.shape[1])
    joff[...] = jnp.broadcast_to(offs[1], joff.shape)

    barrier = pltpu.get_barrier_semaphore()
    for other in (cw, ccw, pair, prev, nxt):
        pl.semaphore_signal(barrier, inc=1, device_id=(other, mj), device_id_type=MESH)
    pl.semaphore_signal(barrier, inc=1, device_id=(me, 1 - mj), device_id_type=MESH)
    pl.semaphore_wait(barrier, 6)

    jitter = pltpu.make_async_remote_copy(
        joff, poff, jit_sem.at[0], jit_sem.at[1], device_id=(nxt, mj), device_id_type=MESH
    )
    jitter.start()

    def lag_of(off_row):
        u = lax.broadcasted_iota(jnp.int32, (SPACING, LANES), 0)
        return u - off_row

    def partial_spectra(off_row, groups_of, fresh=()):
        lag = lag_of(off_row)
        table[...] = rotated(lag, off_row)
        total = jnp.zeros((rows, LANES), jnp.float32)
        for g in groups_of:
            if g in fresh:
                load(g).wait()
            for b in range(GROUP):
                here = lag_of(off_row) + (g * GROUP + b) * SPACING
                inside = (here >= 0) & (here < WIN)
                tmask[pl.ds(b * SPACING, SPACING), :] = jnp.where(inside, table[...], 0.0).astype(
                    jnp.bfloat16
                )
            total = total + jnp.dot(
                rec[:, g * span : (g + 1) * span], tmask[...], preferred_element_type=jnp.float32
            )
        return total

    def ring(src, h, d):
        return pltpu.make_async_remote_copy(
            gat.at[src, h], gat.at[src, h], ring_send.at[d, src, h], chunk_recv.at[src, h],
            device_id=(cw if d == 0 else ccw, mj), device_id_type=MESH,
        )

    def share(src, h):
        return pltpu.make_async_remote_copy(
            gat.at[src, h], gat.at[src, h], pair_send.at[src, h], chunk_recv.at[src, h],
            device_id=(pair, mj), device_id_type=MESH,
        )

    home = me * ncol // rows
    provider = home == mj
    first = pl.multiple_of(jnp.where(provider, me * ncol - home * rows, 0), 16)

    def col_far(src, h):
        return pltpu.make_async_remote_copy(
            gat.at[src, h, pl.ds(first, ncol), :], col.at[src, h], col_send.at[src, h],
            col_recv.at[src, h], device_id=(me, 1 - mj), device_id_type=MESH,
        )

    def col_near(src, h):
        return pltpu.make_async_copy(
            gat.at[src, h, pl.ds(first, ncol), :], col.at[src, h], col_recv.at[src, h]
        )

    def send_col(src, h):
        @pl.when(provider)
        def _():
            col_far(src, h).start()
            col_near(src, h).start()

    def send_own(h):
        ring(me, h, 0).start()
        ring(me, h, 1).start()
        share(me, h).start()
        send_col(me, h)

    def gram(src):
        for h in range(2):
            x = col[src, h].astype(jnp.float32)
            freq, part, _ = lane_fields(x.shape)
            swapped = jnp.where(part == 0, pltpu.roll(x, LANES - 16, 1), -pltpu.roll(x, 16, 1))
            for ri, value in enumerate((x, swapped)):
                for f in range(4):
                    rmat[pl.ds((ri * 4 + f) * ncol, ncol), h * LANES : (h + 1) * LANES] = jnp.where(
                        freq == f, value, 0.0
                    ).astype(jnp.bfloat16)
        left = jnp.concatenate([gat[src, 0], gat[src, 1]], axis=1)
        acc[...] += lax.dot_general(
            rmat[...], left, (((1,), (1,)), ((), ())), preferred_element_type=jnp.float32
        )

    acc[...] = jnp.zeros_like(acc)
    gat[me, 0] = partial_spectra(offs[0], (0, 1, 2), (0, 1, 2)).astype(jnp.bfloat16)
    send_own(0)

    jitter.wait()
    offp = poff[0:1, :] - rec.shape[1]
    foreign = partial_spectra(offp, (0,))
    cut = rows // 2
    rim_out[...] = foreign[:cut] + pltpu.roll(foreign[cut:], LANES - 8, 1)
    rim = pltpu.make_async_remote_copy(
        rim_out, rim_in, rim_sem.at[0], rim_sem.at[1], device_id=(prev, mj), device_id_type=MESH
    )
    rim.start()
    second = partial_spectra(offs[1], (2, 3), (3,))
    rim.wait()
    _, _, shot = lane_fields((cut, LANES))
    wanted = (shot >= 8) & (me < n - 1)
    upper = jnp.where(wanted, rim_in[...], 0.0)
    lower = jnp.where(wanted, pltpu.roll(rim_in[...], 8, 1), 0.0)
    gat[me, 1, :cut] = (second[:cut] + upper).astype(jnp.bfloat16)
    gat[me, 1, cut:] = (second[cut:] + lower).astype(jnp.bfloat16)
    send_own(1)

    half = chips // 2

    def hops(h, d):
        return half if h == d else half - 1

    def arrivals(t):
        found = []
        for h in range(2):
            for d in range(2):
                if 1 <= t <= hops(h, d):
                    found.append((h, d))
        return found

    def source(t, d, which):
        return device_at(pos - t if d == 0 else pos + t, which)

    def step_sources(t):
        if t == 0:
            return [0]
        return [0, 1] if t < half else [0]

    def gram_step(t):
        for which in (core, 1 - core):
            for d in step_sources(t):
                src = source(t, d, which)
                for h in range(2):
                    col_near(src, h).wait()
                gram(src)

    for t in range(half + 1):
        for h, d in arrivals(t):
            src = source(t, d, core)
            ring(src, h, d).wait_recv()
            if t < hops(h, d):
                ring(src, h, d).start()
            share(src, h).start()
            send_col(src, h)
        if t > 0:
            gram_step(t - 1)
        for d in step_sources(t):
            for h in range(2):
                src = source(t, d, 1 - core)
                share(src, h).wait_recv()
                send_col(src, h)
    gram_step(half)

    scale = 1.0 / (n * 2 * HALF)
    for g in range(8):
        out_ref[g // 4, g % 4] = acc[g * ncol : (g + 1) * ncol, :] * scale

    for h in range(2):
        ring(me, h, 0).wait_send()
        ring(me, h, 1).wait_send()
    for t in range(1, half + 1):
        for h, d in arrivals(t):
            src = source(t, d, core)
            if t < hops(h, d):
                ring(src, h, d).wait_send()
            share(src, h).wait_send()
    for h in range(2):
        share(me, h).wait_send()

    @pl.when(provider)
    def _():
        for src in range(n):
            for h in range(2):
                col_far(src, h).wait_send()


def fused_device(n, ncol, record, shot_fire_samples):
    rows, length = record.shape
    gram = pl.pallas_call(
        functools.partial(kernel, n),
        out_shape=jax.ShapeDtypeStruct((2, 4, ncol, rows), jnp.float32),
        in_specs=[
            pl.BlockSpec(memory_space=pltpu.SMEM),
            pl.BlockSpec(memory_space=pl.ANY),
        ],
        out_specs=pl.BlockSpec(memory_space=pltpu.VMEM),
        scratch_shapes=[
            pltpu.VMEM((rows, length), jnp.bfloat16),
            pltpu.VMEM((8, LANES), jnp.int32),
            pltpu.VMEM((8, LANES), jnp.int32),
            pltpu.VMEM((SPACING, LANES), jnp.float32),
            pltpu.VMEM((GROUP * SPACING, LANES), jnp.bfloat16),
            pltpu.VMEM((rows // 2, LANES), jnp.float32),
            pltpu.VMEM((rows // 2, LANES), jnp.float32),
            pltpu.VMEM((n, 2, rows, LANES), jnp.bfloat16),
            pltpu.VMEM((n, 2, ncol, LANES), jnp.bfloat16),
            pltpu.VMEM((8 * ncol, 2 * LANES), jnp.bfloat16),
            pltpu.VMEM((8 * ncol, rows), jnp.float32),
            pltpu.SemaphoreType.DMA((length // (GROUP * SPACING),)),
            pltpu.SemaphoreType.DMA((2,)),
            pltpu.SemaphoreType.DMA((2,)),
            pltpu.SemaphoreType.DMA((2, n, 2)),
            pltpu.SemaphoreType.DMA((n, 2)),
            pltpu.SemaphoreType.DMA((n, 2)),
            pltpu.SemaphoreType.DMA((n, 2)),
            pltpu.SemaphoreType.DMA((n, 2)),
        ],
        compiler_params=pltpu.CompilerParams(
            collective_id=0, has_side_effects=True, vmem_limit_bytes=59 * 1024 * 1024
        ),
    )(shot_fire_samples, record)
    return gram.transpose(0, 1, 3, 2)


def whole_step(n, receivers, record, shot_fire_samples):
    rows, length = record.shape
    shots = shot_fire_samples.shape[0]
    ncol = receivers // n
    fits = (
        receivers == 2 * rows and ncol % 16 == 0 and rows % (2 * ncol) == 0
        and shots == 2 * HALF and length == shots * SPACING and n % 8 == 0
    )
    if fits:
        return fused_device(n, ncol, record, shot_fire_samples)
    return per_device(record, shot_fire_samples)


def solution(mesh):
    def step(record, shot_fire_samples):
        body = functools.partial(whole_step, mesh.shape["shot"], record.shape[0])
        return jax.shard_map(
            body,
            mesh=mesh,
            in_specs=(P("rcv", "shot"), P("shot")),
            out_specs=P(None, None, "rcv", "shot"),
            check_vma=False,
        )(record, shot_fire_samples)

    return step
```

```python
import functools
import math

import jax
import jax.numpy as jnp
from jax import lax
from jax.experimental import pallas as pl
from jax.experimental.pallas import tpu as pltpu
from jax.sharding import PartitionSpec as P

WIN = 2048
SPACING = 256


freq_bins = (24, 40, 56, 80)


def shifted(block, axis, distance):
    devices = range(lax.axis_size(axis))
    route = [(i - distance, i) for i in devices if i - distance in devices]
    return lax.ppermute(block, axis, route)


def dft_table(window_len):
    lag_index = jnp.arange(window_len, dtype=jnp.int32)
    bin_list = jnp.array(freq_bins, dtype=jnp.int32)
    turn_count = lag_index[:, None] * bin_list[None, :] % window_len
    phase_angle = 2.0 * math.pi / window_len * turn_count.astype(jnp.float32)
    dft_rows = jnp.concatenate([jnp.cos(phase_angle), -jnp.sin(phase_angle)], axis=1) / math.sqrt(
        window_len
    )
    return dft_rows.astype(jnp.bfloat16)


def shifted_tables(jitter, span):
    lag_index = jnp.arange(span, dtype=jnp.int32)[None, :] - jitter[:, None]
    inside = (lag_index >= 0) & (lag_index < WIN)
    clipped = jnp.clip(lag_index, 0, WIN - 1)
    bin_list = jnp.array(freq_bins, dtype=jnp.int32)
    turn_count = clipped[:, None, :] * bin_list[None, :, None] % WIN
    phase_angle = 2.0 * math.pi / WIN * turn_count.astype(jnp.float32)
    table = jnp.concatenate([jnp.cos(phase_angle), -jnp.sin(phase_angle)], axis=1) / math.sqrt(WIN)
    table = jnp.where(inside[:, None, :], table, 0.0)
    return table.astype(jnp.bfloat16)


def local_spectra(extended, sample_offsets, dft_rows):
    count_of_shots = sample_offsets.shape[0]
    reach_blocks = WIN // SPACING + 1
    jitter = sample_offsets - jnp.arange(count_of_shots, dtype=jnp.int32) * SPACING
    tables = shifted_tables(jitter, reach_blocks * SPACING)
    tables = tables.reshape(count_of_shots, dft_rows.shape[1], reach_blocks, SPACING)
    blocks = extended.reshape(extended.shape[0], extended.shape[1] // SPACING, SPACING)
    total = jnp.zeros((count_of_shots, dft_rows.shape[1], extended.shape[0]), jnp.float32)
    for offset in range(reach_blocks):
        record_part = blocks[:, offset : offset + count_of_shots, :]
        total = total + jnp.einsum(
            "rsu,scu->scr", record_part, tables[:, :, offset, :], preferred_element_type=jnp.float32
        )
    return total


def gram_terms(left, right):
    nfreq = len(freq_bins)
    left_re = left[:, :nfreq, :]
    left_im = left[:, nfreq:, :]
    right_re = right[:, :nfreq, :]
    right_im = right[:, nfreq:, :]
    gram_real = jnp.einsum("sfr,sfq->frq", left_re, right_re, preferred_element_type=jnp.float32)
    gram_real = gram_real + jnp.einsum(
        "sfr,sfq->frq", left_im, right_im, preferred_element_type=jnp.float32
    )
    gram_imag = jnp.einsum("sfr,sfq->frq", left_re, right_im, preferred_element_type=jnp.float32)
    gram_imag = gram_imag - jnp.einsum(
        "sfr,sfq->frq", left_im, right_re, preferred_element_type=jnp.float32
    )
    return jnp.stack([gram_real, gram_imag], axis=0)


def per_device(record, shot_fire_samples):
    trace_segment_length = record.shape[1]
    count_of_shots = shot_fire_samples.shape[0]
    dft_rows = dft_table(WIN)
    sample_offsets = shot_fire_samples - lax.axis_index("shot") * trace_segment_length
    head_rows = record[:, :WIN]
    rim_rows = shifted(head_rows, "shot", -1)
    extended = jnp.concatenate([record, rim_rows], axis=1)
    trace_spectra = local_spectra(extended, sample_offsets, dft_rows)
    trace_spectra = trace_spectra.astype(jnp.bfloat16)
    all_receivers = lax.all_gather(trace_spectra, "rcv", axis=2, tiled=True)
    total_shots = count_of_shots * lax.axis_size("shot")
    row_side = lax.all_gather(trace_spectra, "shot", axis=0, tiled=True)
    column_side = lax.all_to_all(all_receivers, "shot", split_axis=2, concat_axis=0, tiled=True)
    result = gram_terms(row_side, column_side)
    return result / total_shots


LANES = 128
HALF = 16
GROUP = 8
MESH = pl.DeviceIdType.MESH


def lane_fields(shape):
    lane = lax.broadcasted_iota(jnp.int32, shape, len(shape) - 1)
    return lane // 32 % 4, lane // 16 % 2, lane % 16


def rotated(lag):
    freq, part, _ = lane_fields((1, LANES))
    bins = jnp.full((1, LANES), freq_bins[0], jnp.int32)
    for f in range(1, len(freq_bins)):
        bins = jnp.where(freq == f, freq_bins[f], bins)
    turn = (lag & (SPACING - 1)) * bins + part * (WIN // 4)
    turn = ((turn + WIN // 2) & (WIN - 1)) - WIN // 2
    x = (math.pi / WIN) * turn.astype(jnp.float32)
    y = x * x
    series = 1.0 / math.factorial(13)
    for k in (11, 9, 7, 5, 3, 1):
        series = series * y + (-1.0) ** (k // 2) / math.factorial(k)
    half_sine = x * series
    return (1.0 - 2.0 * half_sine * half_sine) / math.sqrt(WIN)


def kernel(
    n, fire_ref, rec_ref, out_ref,
    rec, joff, poff, table, tmask, rim_out, rim_in, gat, col, rmat, acc,
    rec_sem, jit_sem, rim_sem, ring_send, pair_send, chunk_recv, col_send, col_recv,
):
    me = lax.axis_index("shot")
    mj = lax.axis_index("rcv")
    rows = rec.shape[0]
    span = GROUP * SPACING
    chips = n // 2
    nz = chips // 2
    ncol = col.shape[2]
    shift, reach = SPACING.bit_length() - 1, WIN // SPACING
    core = me % 2
    chip = me // 2
    z, y = chip // 2, chip % 2
    pos = jnp.where(y == 0, z, chips - 1 - z)

    def device_at(position, which):
        q = (position + 2 * chips) % chips
        second = q >= nz
        zz = jnp.where(second, chips - 1 - q, q)
        yy = jnp.where(second, 1, 0)
        return (zz * 2 + yy) * 2 + which

    cw, ccw = device_at(pos + 1, core), device_at(pos - 1, core)
    pair = chip * 2 + (1 - core)
    prev, nxt = (me + n - 1) % n, (me + 1) % n

    def load(g):
        part = pl.ds(g * span, span)
        return pltpu.make_async_copy(rec_ref.at[:, part], rec.at[:, part], rec_sem.at[g])

    for g in (1, 2, 0, 3):
        load(g).start()

    _, _, shot_lane = lane_fields((1, LANES))
    offs = []
    for h in range(2):
        row = jnp.zeros((1, LANES), jnp.int32)
        for s in range(HALF):
            row = jnp.where(shot_lane == s, fire_ref[h * HALF + s], row)
        offs.append(row - me * rec.shape[1])
    joff[...] = jnp.broadcast_to(offs[1], joff.shape)

    barrier = pltpu.get_barrier_semaphore()
    for other in (cw, ccw, pair, prev, nxt):
        pl.semaphore_signal(barrier, inc=1, device_id=(other, mj), device_id_type=MESH)
    pl.semaphore_signal(barrier, inc=1, device_id=(me, 1 - mj), device_id_type=MESH)
    pl.semaphore_wait(barrier, 6)

    jitter = pltpu.make_async_remote_copy(
        joff, poff, jit_sem.at[0], jit_sem.at[1], device_id=(nxt, mj), device_id_type=MESH
    )
    jitter.start()

    def fill_tables(kind, off_row):
        u = lax.broadcasted_iota(jnp.int32, (SPACING, LANES), 0)
        start = off_row & (SPACING - 1)
        value = rotated(u - start)
        table[kind, 0] = jnp.where(u >= start, value, 0.0).astype(jnp.bfloat16)
        table[kind, 1] = jnp.where(u < start, value, 0.0).astype(jnp.bfloat16)

    def group_dot(g, kinds):
        for slot, (kind, off_row) in enumerate(kinds):
            block_of = jnp.broadcast_to(off_row >> shift, (16, LANES))
            lanes = slice(slot * LANES, (slot + 1) * LANES)
            for b in range(GROUP):
                order = g * GROUP + b - block_of
                early = ((order >= 0) & (order < reach)).astype(jnp.float32).astype(jnp.bfloat16)
                late = ((order >= 1) & (order <= reach)).astype(jnp.float32).astype(jnp.bfloat16)
                block = (SPACING // 16, 16, LANES)
                mixed = table[kind, 0].reshape(block) * early + table[kind, 1].reshape(block) * late
                tmask[b * SPACING : (b + 1) * SPACING, lanes] = mixed.reshape(SPACING, LANES)
        return jnp.dot(
            rec[:, g * span : (g + 1) * span], tmask[:, : len(kinds) * LANES],
            preferred_element_type=jnp.float32,
        )

    def ring(src, h, d):
        return pltpu.make_async_remote_copy(
            gat.at[src, h], gat.at[src, h], ring_send.at[d, src, h], chunk_recv.at[src, h],
            device_id=(cw if d == 0 else ccw, mj), device_id_type=MESH,
        )

    def share(src, h):
        return pltpu.make_async_remote_copy(
            gat.at[src, h], gat.at[src, h], pair_send.at[src, h], chunk_recv.at[src, h],
            device_id=(pair, mj), device_id_type=MESH,
        )

    home = me * ncol // rows
    provider = home == mj
    first = pl.multiple_of(jnp.where(provider, me * ncol - home * rows, 0), 16)

    def col_far(src, h):
        return pltpu.make_async_remote_copy(
            gat.at[src, h, pl.ds(first, ncol), :], col.at[src, h], col_send.at[src, h],
            col_recv.at[src, h], device_id=(me, 1 - mj), device_id_type=MESH,
        )

    def col_near(src, h):
        return pltpu.make_async_copy(
            gat.at[src, h, pl.ds(first, ncol), :], col.at[src, h], col_recv.at[src, h]
        )

    def send_col(src, h):
        @pl.when(provider)
        def _():
            col_far(src, h).start()
            col_near(src, h).start()

    def send_own(h):
        ring(me, h, 0).start()
        ring(me, h, 1).start()
        share(me, h).start()
        send_col(me, h)

    def gram(src):
        for h in range(2):
            x = col[src, h].astype(jnp.float32)
            freq, part, _ = lane_fields(x.shape)
            swapped = jnp.where(part == 0, pltpu.roll(x, LANES - 16, 1), -pltpu.roll(x, 16, 1))
            for ri, value in enumerate((x, swapped)):
                for f in range(4):
                    rmat[pl.ds((ri * 4 + f) * ncol, ncol), h * LANES : (h + 1) * LANES] = jnp.where(
                        freq == f, value, 0.0
                    ).astype(jnp.bfloat16)
        left = jnp.concatenate([gat[src, 0], gat[src, 1]], axis=1)
        acc[...] += lax.dot_general(
            rmat[...], left, (((1,), (1,)), ((), ())), preferred_element_type=jnp.float32
        )

    fill_tables(0, offs[0])
    fill_tables(1, offs[1])
    acc[...] = jnp.zeros_like(acc)
    kinds = ((0, offs[0]), (1, offs[1]))
    load(1).wait()
    own = group_dot(1, kinds[:1])
    load(2).wait()
    both = group_dot(2, kinds)
    jitter.wait()
    offp = poff[0:1, :] - rec.shape[1]
    fill_tables(2, offp)
    load(0).wait()
    head = group_dot(0, (kinds[0], (2, offp)))
    gat[me, 0] = (own + both[:, :LANES] + head[:, :LANES]).astype(jnp.bfloat16)
    send_own(0)
    foreign = head[:, LANES:]
    cut = rows // 2
    rim_out[...] = foreign[:cut] + pltpu.roll(foreign[cut:], LANES - 8, 1)
    rim = pltpu.make_async_remote_copy(
        rim_out, rim_in, rim_sem.at[0], rim_sem.at[1], device_id=(prev, mj), device_id_type=MESH
    )
    rim.start()
    load(3).wait()
    second = both[:, LANES:] + group_dot(3, kinds[1:])
    rim.wait()
    _, _, shot = lane_fields((cut, LANES))
    wanted = (shot >= 8) & (me < n - 1)
    upper = jnp.where(wanted, rim_in[...], 0.0)
    lower = jnp.where(wanted, pltpu.roll(rim_in[...], 8, 1), 0.0)
    gat[me, 1, :cut] = (second[:cut] + upper).astype(jnp.bfloat16)
    gat[me, 1, cut:] = (second[cut:] + lower).astype(jnp.bfloat16)
    send_own(1)

    half = chips // 2

    def hops(h, d):
        return half if h == d else half - 1

    def arrivals(t):
        found = []
        for h in range(2):
            for d in range(2):
                if 1 <= t <= hops(h, d):
                    found.append((h, d))
        return found

    def source(t, d, which):
        return device_at(pos - t if d == 0 else pos + t, which)

    def step_sources(t):
        if t == 0:
            return [0]
        return [0, 1] if t < half else [0]

    def gram_step(t):
        for which in (core, 1 - core):
            for d in step_sources(t):
                src = source(t, d, which)
                for h in range(2):
                    col_near(src, h).wait()
                gram(src)

    for t in range(half + 1):
        for h, d in arrivals(t):
            src = source(t, d, core)
            ring(src, h, d).wait_recv()
            if t < hops(h, d):
                ring(src, h, d).start()
            share(src, h).start()
            send_col(src, h)
        if t > 0:
            gram_step(t - 1)
        for d in step_sources(t):
            for h in range(2):
                src = source(t, d, 1 - core)
                share(src, h).wait_recv()
                send_col(src, h)
    gram_step(half)

    scale = 1.0 / (n * 2 * HALF)
    for g in range(8):
        out_ref[g // 4, g % 4] = acc[g * ncol : (g + 1) * ncol, :] * scale

    for h in range(2):
        ring(me, h, 0).wait_send()
        ring(me, h, 1).wait_send()
    for t in range(1, half + 1):
        for h, d in arrivals(t):
            src = source(t, d, core)
            if t < hops(h, d):
                ring(src, h, d).wait_send()
            share(src, h).wait_send()
    for h in range(2):
        share(me, h).wait_send()

    @pl.when(provider)
    def _():
        for src in range(n):
            for h in range(2):
                col_far(src, h).wait_send()


def fused_device(n, ncol, record, shot_fire_samples):
    rows, length = record.shape
    gram = pl.pallas_call(
        functools.partial(kernel, n),
        out_shape=jax.ShapeDtypeStruct((2, 4, ncol, rows), jnp.float32),
        in_specs=[
            pl.BlockSpec(memory_space=pltpu.SMEM),
            pl.BlockSpec(memory_space=pl.ANY),
        ],
        out_specs=pl.BlockSpec(memory_space=pltpu.VMEM),
        scratch_shapes=[
            pltpu.VMEM((rows, length), jnp.bfloat16),
            pltpu.VMEM((8, LANES), jnp.int32),
            pltpu.VMEM((8, LANES), jnp.int32),
            pltpu.VMEM((3, 2, SPACING, LANES), jnp.bfloat16),
            pltpu.VMEM((GROUP * SPACING, 2 * LANES), jnp.bfloat16),
            pltpu.VMEM((rows // 2, LANES), jnp.float32),
            pltpu.VMEM((rows // 2, LANES), jnp.float32),
            pltpu.VMEM((n, 2, rows, LANES), jnp.bfloat16),
            pltpu.VMEM((n, 2, ncol, LANES), jnp.bfloat16),
            pltpu.VMEM((8 * ncol, 2 * LANES), jnp.bfloat16),
            pltpu.VMEM((8 * ncol, rows), jnp.float32),
            pltpu.SemaphoreType.DMA((length // (GROUP * SPACING),)),
            pltpu.SemaphoreType.DMA((2,)),
            pltpu.SemaphoreType.DMA((2,)),
            pltpu.SemaphoreType.DMA((2, n, 2)),
            pltpu.SemaphoreType.DMA((n, 2)),
            pltpu.SemaphoreType.DMA((n, 2)),
            pltpu.SemaphoreType.DMA((n, 2)),
            pltpu.SemaphoreType.DMA((n, 2)),
        ],
        compiler_params=pltpu.CompilerParams(
            collective_id=0, has_side_effects=True, vmem_limit_bytes=56 * 1024 * 1024
        ),
    )(shot_fire_samples, record)
    return gram.transpose(0, 1, 3, 2)


def whole_step(n, receivers, record, shot_fire_samples):
    rows, length = record.shape
    shots = shot_fire_samples.shape[0]
    ncol = receivers // n
    fits = (
        receivers == 2 * rows and ncol % 16 == 0 and rows % (2 * ncol) == 0
        and shots == 2 * HALF and length == shots * SPACING and n % 8 == 0
    )
    if fits:
        return fused_device(n, ncol, record, shot_fire_samples)
    return per_device(record, shot_fire_samples)


def solution(mesh):
    def step(record, shot_fire_samples):
        body = functools.partial(whole_step, mesh.shape["shot"], record.shape[0])
        return jax.shard_map(
            body,
            mesh=mesh,
            in_specs=(P("rcv", "shot"), P("shot")),
            out_specs=P(None, None, "rcv", "shot"),
            check_vma=False,
        )(record, shot_fire_samples)

    return step
```

```python
import functools
import math

import jax
import jax.numpy as jnp
from jax import lax
from jax.experimental import pallas as pl
from jax.experimental.pallas import tpu as pltpu
from jax.sharding import PartitionSpec as P

WIN = 2048
SPACING = 256


freq_bins = (24, 40, 56, 80)


def shifted(block, axis, distance):
    devices = range(lax.axis_size(axis))
    route = [(i - distance, i) for i in devices if i - distance in devices]
    return lax.ppermute(block, axis, route)


def dft_table(window_len):
    lag_index = jnp.arange(window_len, dtype=jnp.int32)
    bin_list = jnp.array(freq_bins, dtype=jnp.int32)
    turn_count = lag_index[:, None] * bin_list[None, :] % window_len
    phase_angle = 2.0 * math.pi / window_len * turn_count.astype(jnp.float32)
    dft_rows = jnp.concatenate([jnp.cos(phase_angle), -jnp.sin(phase_angle)], axis=1) / math.sqrt(
        window_len
    )
    return dft_rows.astype(jnp.bfloat16)


def shifted_tables(jitter, span):
    lag_index = jnp.arange(span, dtype=jnp.int32)[None, :] - jitter[:, None]
    inside = (lag_index >= 0) & (lag_index < WIN)
    clipped = jnp.clip(lag_index, 0, WIN - 1)
    bin_list = jnp.array(freq_bins, dtype=jnp.int32)
    turn_count = clipped[:, None, :] * bin_list[None, :, None] % WIN
    phase_angle = 2.0 * math.pi / WIN * turn_count.astype(jnp.float32)
    table = jnp.concatenate([jnp.cos(phase_angle), -jnp.sin(phase_angle)], axis=1) / math.sqrt(WIN)
    table = jnp.where(inside[:, None, :], table, 0.0)
    return table.astype(jnp.bfloat16)


def local_spectra(extended, sample_offsets, dft_rows):
    count_of_shots = sample_offsets.shape[0]
    reach_blocks = WIN // SPACING + 1
    jitter = sample_offsets - jnp.arange(count_of_shots, dtype=jnp.int32) * SPACING
    tables = shifted_tables(jitter, reach_blocks * SPACING)
    tables = tables.reshape(count_of_shots, dft_rows.shape[1], reach_blocks, SPACING)
    blocks = extended.reshape(extended.shape[0], extended.shape[1] // SPACING, SPACING)
    total = jnp.zeros((count_of_shots, dft_rows.shape[1], extended.shape[0]), jnp.float32)
    for offset in range(reach_blocks):
        record_part = blocks[:, offset : offset + count_of_shots, :]
        total = total + jnp.einsum(
            "rsu,scu->scr", record_part, tables[:, :, offset, :], preferred_element_type=jnp.float32
        )
    return total


def gram_terms(left, right):
    nfreq = len(freq_bins)
    left_re = left[:, :nfreq, :]
    left_im = left[:, nfreq:, :]
    right_re = right[:, :nfreq, :]
    right_im = right[:, nfreq:, :]
    gram_real = jnp.einsum("sfr,sfq->frq", left_re, right_re, preferred_element_type=jnp.float32)
    gram_real = gram_real + jnp.einsum(
        "sfr,sfq->frq", left_im, right_im, preferred_element_type=jnp.float32
    )
    gram_imag = jnp.einsum("sfr,sfq->frq", left_re, right_im, preferred_element_type=jnp.float32)
    gram_imag = gram_imag - jnp.einsum(
        "sfr,sfq->frq", left_im, right_re, preferred_element_type=jnp.float32
    )
    return jnp.stack([gram_real, gram_imag], axis=0)


def per_device(record, shot_fire_samples):
    trace_segment_length = record.shape[1]
    count_of_shots = shot_fire_samples.shape[0]
    dft_rows = dft_table(WIN)
    sample_offsets = shot_fire_samples - lax.axis_index("shot") * trace_segment_length
    head_rows = record[:, :WIN]
    rim_rows = shifted(head_rows, "shot", -1)
    extended = jnp.concatenate([record, rim_rows], axis=1)
    trace_spectra = local_spectra(extended, sample_offsets, dft_rows)
    trace_spectra = trace_spectra.astype(jnp.bfloat16)
    all_receivers = lax.all_gather(trace_spectra, "rcv", axis=2, tiled=True)
    total_shots = count_of_shots * lax.axis_size("shot")
    row_side = lax.all_gather(trace_spectra, "shot", axis=0, tiled=True)
    column_side = lax.all_to_all(all_receivers, "shot", split_axis=2, concat_axis=0, tiled=True)
    result = gram_terms(row_side, column_side)
    return result / total_shots


LANES = 128
HALF = 16
GROUP = 8
MESH = pl.DeviceIdType.MESH


def lane_fields(shape):
    lane = lax.broadcasted_iota(jnp.int32, shape, len(shape) - 1)
    return lane // 32 % 4, lane // 16 % 2, lane % 16


def rotated(lag):
    freq, part, _ = lane_fields((1, LANES))
    bins = jnp.full((1, LANES), freq_bins[0], jnp.int32)
    for f in range(1, len(freq_bins)):
        bins = jnp.where(freq == f, freq_bins[f], bins)
    turn = (lag & (SPACING - 1)) * bins + part * (WIN // 4)
    turn = ((turn + WIN // 2) & (WIN - 1)) - WIN // 2
    x = (math.pi / WIN) * turn.astype(jnp.float32)
    y = x * x
    series = 1.0 / math.factorial(13)
    for k in (11, 9, 7, 5, 3, 1):
        series = series * y + (-1.0) ** (k // 2) / math.factorial(k)
    half_sine = x * series
    return (1.0 - 2.0 * half_sine * half_sine) / math.sqrt(WIN)


def kernel(
    n, fire_hbm, rec_ref, out_ref,
    fire_ref, fire_sem, rec, joff, poff, table, tmask, rim_out, rim_in, gat, col, rmat, acc,
    rec_sem, jit_sem, rim_sem, ring_send, pair_send, chunk_recv, col_send, col_recv,
):
    me = lax.axis_index("shot")
    mj = lax.axis_index("rcv")
    rows = rec.shape[0]
    span = GROUP * SPACING
    chips = n // 2
    nz = chips // 2
    ncol = col.shape[2]
    shift, reach = SPACING.bit_length() - 1, WIN // SPACING
    core = me % 2
    chip = me // 2
    z, y = chip // 2, chip % 2
    pos = jnp.where(y == 0, z, chips - 1 - z)

    def device_at(position, which):
        q = (position + 2 * chips) % chips
        second = q >= nz
        zz = jnp.where(second, chips - 1 - q, q)
        yy = jnp.where(second, 1, 0)
        return (zz * 2 + yy) * 2 + which

    cw, ccw = device_at(pos + 1, core), device_at(pos - 1, core)
    pair = chip * 2 + (1 - core)
    prev, nxt = (me + n - 1) % n, (me + 1) % n

    def load(g):
        part = pl.ds(g * span, span)
        return pltpu.make_async_copy(rec_ref.at[:, part], rec.at[:, part], rec_sem.at[g])

    fires = pltpu.make_async_copy(fire_hbm, fire_ref, fire_sem)
    fires.start()
    for g in (1, 2, 0, 3):
        load(g).start()

    barrier = pltpu.get_barrier_semaphore()
    for other in (cw, ccw, pair, prev, nxt):
        pl.semaphore_signal(barrier, inc=1, device_id=(other, mj), device_id_type=MESH)
    pl.semaphore_signal(barrier, inc=1, device_id=(me, 1 - mj), device_id_type=MESH)
    fires.wait()
    _, _, shot_lane = lane_fields((1, LANES))
    offs = []
    for h in range(2):
        row = jnp.zeros((1, LANES), jnp.int32)
        for s in range(HALF):
            row = jnp.where(shot_lane == s, fire_ref[h * HALF + s], row)
        offs.append(row - me * rec.shape[1])
    joff[...] = jnp.broadcast_to(offs[1], joff.shape)

    jitter = pltpu.make_async_remote_copy(
        joff, poff, jit_sem.at[0], jit_sem.at[1], device_id=(nxt, mj), device_id_type=MESH
    )

    def fill_tables(kind, off_row):
        u = lax.broadcasted_iota(jnp.int32, (SPACING, LANES), 0)
        start = off_row & (SPACING - 1)
        value = rotated(u - start)
        table[kind, 0] = jnp.where(u >= start, value, 0.0).astype(jnp.bfloat16)
        table[kind, 1] = jnp.where(u < start, value, 0.0).astype(jnp.bfloat16)

    def group_dot(g, kinds):
        for slot, (kind, off_row) in enumerate(kinds):
            block_of = jnp.broadcast_to(off_row >> shift, (16, LANES))
            lanes = slice(slot * LANES, (slot + 1) * LANES)
            for b in range(GROUP):
                order = g * GROUP + b - block_of
                early = ((order >= 0) & (order < reach)).astype(jnp.float32).astype(jnp.bfloat16)
                late = ((order >= 1) & (order <= reach)).astype(jnp.float32).astype(jnp.bfloat16)
                block = (SPACING // 16, 16, LANES)
                mixed = table[kind, 0].reshape(block) * early + table[kind, 1].reshape(block) * late
                tmask[b * SPACING : (b + 1) * SPACING, lanes] = mixed.reshape(SPACING, LANES)
        return jnp.dot(
            rec[:, g * span : (g + 1) * span], tmask[:, : len(kinds) * LANES],
            preferred_element_type=jnp.float32,
        )

    def ring(src, h, d):
        return pltpu.make_async_remote_copy(
            gat.at[src, h], gat.at[src, h], ring_send.at[d, src, h], chunk_recv.at[src, h],
            device_id=(cw if d == 0 else ccw, mj), device_id_type=MESH,
        )

    def share(src, h):
        return pltpu.make_async_remote_copy(
            gat.at[src, h], gat.at[src, h], pair_send.at[src, h], chunk_recv.at[src, h],
            device_id=(pair, mj), device_id_type=MESH,
        )

    home = me * ncol // rows
    provider = home == mj
    first = pl.multiple_of(jnp.where(provider, me * ncol - home * rows, 0), 16)

    def col_far(src, h):
        return pltpu.make_async_remote_copy(
            gat.at[src, h, pl.ds(first, ncol), :], col.at[src, h], col_send.at[src, h],
            col_recv.at[src, h], device_id=(me, 1 - mj), device_id_type=MESH,
        )

    def col_near(src, h):
        return pltpu.make_async_copy(
            gat.at[src, h, pl.ds(first, ncol), :], col.at[src, h], col_recv.at[src, h]
        )

    def send_col(src, h):
        @pl.when(provider)
        def _():
            col_far(src, h).start()
            col_near(src, h).start()

    def send_own(h):
        ring(me, h, 0).start()
        ring(me, h, 1).start()
        share(me, h).start()
        send_col(me, h)

    def gram(src):
        for h in range(2):
            x = col[src, h].astype(jnp.float32)
            freq, part, _ = lane_fields(x.shape)
            swapped = jnp.where(part == 0, pltpu.roll(x, LANES - 16, 1), -pltpu.roll(x, 16, 1))
            for ri, value in enumerate((x, swapped)):
                for f in range(4):
                    rmat[pl.ds((ri * 4 + f) * ncol, ncol), h * LANES : (h + 1) * LANES] = jnp.where(
                        freq == f, value, 0.0
                    ).astype(jnp.bfloat16)
        left = jnp.concatenate([gat[src, 0], gat[src, 1]], axis=1)
        acc[...] += lax.dot_general(
            rmat[...], left, (((1,), (1,)), ((), ())), preferred_element_type=jnp.float32
        )

    fill_tables(0, offs[0])
    fill_tables(1, offs[1])
    acc[...] = jnp.zeros_like(acc)
    kinds = ((0, offs[0]), (1, offs[1]))
    load(1).wait()
    own = group_dot(1, kinds[:1])
    pl.semaphore_wait(barrier, 6)
    jitter.start()
    load(2).wait()
    both = group_dot(2, kinds)
    load(0).wait()
    own = own + both[:, :LANES] + group_dot(0, kinds[:1])
    gat[me, 0] = own.astype(jnp.bfloat16)
    send_own(0)
    jitter.wait()
    offp = poff[0:1, :] - rec.shape[1]
    fill_tables(2, offp)
    foreign = group_dot(0, ((2, offp),))
    cut = rows // 2
    rim_out[...] = foreign[:cut] + pltpu.roll(foreign[cut:], LANES - 8, 1)
    rim = pltpu.make_async_remote_copy(
        rim_out, rim_in, rim_sem.at[0], rim_sem.at[1], device_id=(prev, mj), device_id_type=MESH
    )
    rim.start()
    load(3).wait()
    second = both[:, LANES:] + group_dot(3, kinds[1:])
    rim.wait()
    _, _, shot = lane_fields((cut, LANES))
    wanted = (shot >= 8) & (me < n - 1)
    upper = jnp.where(wanted, rim_in[...], 0.0)
    lower = jnp.where(wanted, pltpu.roll(rim_in[...], 8, 1), 0.0)
    gat[me, 1, :cut] = (second[:cut] + upper).astype(jnp.bfloat16)
    gat[me, 1, cut:] = (second[cut:] + lower).astype(jnp.bfloat16)
    send_own(1)

    half = chips // 2

    def hops(h, d):
        return half if h == d else half - 1

    def arrivals(t):
        found = []
        for h in range(2):
            for d in range(2):
                if 1 <= t <= hops(h, d):
                    found.append((h, d))
        return found

    def source(t, d, which):
        return device_at(pos - t if d == 0 else pos + t, which)

    def step_sources(t):
        if t == 0:
            return [0]
        return [0, 1] if t < half else [0]

    def gram_step(t):
        for which in (core, 1 - core):
            for d in step_sources(t):
                src = source(t, d, which)
                for h in range(2):
                    col_near(src, h).wait()
                gram(src)

    for t in range(half + 1):
        for h, d in arrivals(t):
            src = source(t, d, core)
            ring(src, h, d).wait_recv()
            if t < hops(h, d):
                ring(src, h, d).start()
            share(src, h).start()
            send_col(src, h)
        if t > 0:
            gram_step(t - 1)
        for d in step_sources(t):
            for h in range(2):
                src = source(t, d, 1 - core)
                share(src, h).wait_recv()
                send_col(src, h)
    gram_step(half)

    scale = 1.0 / (n * 2 * HALF)
    for g in range(8):
        out_ref[g // 4, g % 4] = acc[g * ncol : (g + 1) * ncol, :] * scale

    for h in range(2):
        ring(me, h, 0).wait_send()
        ring(me, h, 1).wait_send()
    for t in range(1, half + 1):
        for h, d in arrivals(t):
            src = source(t, d, core)
            if t < hops(h, d):
                ring(src, h, d).wait_send()
            share(src, h).wait_send()
    for h in range(2):
        share(me, h).wait_send()

    @pl.when(provider)
    def _():
        for src in range(n):
            for h in range(2):
                col_far(src, h).wait_send()


def fused_device(n, ncol, record, shot_fire_samples):
    rows, length = record.shape
    gram = pl.pallas_call(
        functools.partial(kernel, n),
        out_shape=jax.ShapeDtypeStruct((2, 4, ncol, rows), jnp.float32),
        in_specs=[
            pl.BlockSpec(memory_space=pltpu.HBM),
            pl.BlockSpec(memory_space=pltpu.HBM),
        ],
        out_specs=pl.BlockSpec(memory_space=pltpu.VMEM),
        scratch_shapes=[
            pltpu.SMEM(shot_fire_samples.shape, jnp.int32),
            pltpu.SemaphoreType.DMA,
            pltpu.VMEM((rows, length), jnp.bfloat16),
            pltpu.VMEM((8, LANES), jnp.int32),
            pltpu.VMEM((8, LANES), jnp.int32),
            pltpu.VMEM((3, 2, SPACING, LANES), jnp.bfloat16),
            pltpu.VMEM((GROUP * SPACING, 2 * LANES), jnp.bfloat16),
            pltpu.VMEM((rows // 2, LANES), jnp.float32),
            pltpu.VMEM((rows // 2, LANES), jnp.float32),
            pltpu.VMEM((n, 2, rows, LANES), jnp.bfloat16),
            pltpu.VMEM((n, 2, ncol, LANES), jnp.bfloat16),
            pltpu.VMEM((8 * ncol, 2 * LANES), jnp.bfloat16),
            pltpu.VMEM((8 * ncol, rows), jnp.float32),
            pltpu.SemaphoreType.DMA((length // (GROUP * SPACING),)),
            pltpu.SemaphoreType.DMA((2,)),
            pltpu.SemaphoreType.DMA((2,)),
            pltpu.SemaphoreType.DMA((2, n, 2)),
            pltpu.SemaphoreType.DMA((n, 2)),
            pltpu.SemaphoreType.DMA((n, 2)),
            pltpu.SemaphoreType.DMA((n, 2)),
            pltpu.SemaphoreType.DMA((n, 2)),
        ],
        compiler_params=pltpu.CompilerParams(
            collective_id=0, has_side_effects=True, vmem_limit_bytes=50 * 1024 * 1024
        ),
    )(shot_fire_samples, record)
    return gram.transpose(0, 1, 3, 2)


def whole_step(n, receivers, record, shot_fire_samples):
    rows, length = record.shape
    shots = shot_fire_samples.shape[0]
    ncol = receivers // n
    fits = (
        receivers == 2 * rows and ncol % 16 == 0 and rows % (2 * ncol) == 0
        and shots == 2 * HALF and length == shots * SPACING and n % 8 == 0
    )
    if fits:
        return fused_device(n, ncol, record, shot_fire_samples)
    return per_device(record, shot_fire_samples)


def solution(mesh):
    def step(record, shot_fire_samples):
        body = functools.partial(whole_step, mesh.shape["shot"], record.shape[0])
        return jax.shard_map(
            body,
            mesh=mesh,
            in_specs=(P("rcv", "shot"), P("shot")),
            out_specs=P(None, None, "rcv", "shot"),
            check_vma=False,
        )(record, shot_fire_samples)

    return step
```

```python
import functools
import math

import jax
import jax.numpy as jnp
from jax import lax
from jax.experimental import pallas as pl
from jax.experimental.pallas import tpu as pltpu
from jax.sharding import PartitionSpec as P

WIN = 2048
SPACING = 256


freq_bins = (24, 40, 56, 80)


def shifted(block, axis, distance):
    devices = range(lax.axis_size(axis))
    route = [(i - distance, i) for i in devices if i - distance in devices]
    return lax.ppermute(block, axis, route)


def dft_table(window_len):
    lag_index = jnp.arange(window_len, dtype=jnp.int32)
    bin_list = jnp.array(freq_bins, dtype=jnp.int32)
    turn_count = lag_index[:, None] * bin_list[None, :] % window_len
    phase_angle = 2.0 * math.pi / window_len * turn_count.astype(jnp.float32)
    dft_rows = jnp.concatenate([jnp.cos(phase_angle), -jnp.sin(phase_angle)], axis=1) / math.sqrt(
        window_len
    )
    return dft_rows.astype(jnp.bfloat16)


def shifted_tables(jitter, span):
    lag_index = jnp.arange(span, dtype=jnp.int32)[None, :] - jitter[:, None]
    inside = (lag_index >= 0) & (lag_index < WIN)
    clipped = jnp.clip(lag_index, 0, WIN - 1)
    bin_list = jnp.array(freq_bins, dtype=jnp.int32)
    turn_count = clipped[:, None, :] * bin_list[None, :, None] % WIN
    phase_angle = 2.0 * math.pi / WIN * turn_count.astype(jnp.float32)
    table = jnp.concatenate([jnp.cos(phase_angle), -jnp.sin(phase_angle)], axis=1) / math.sqrt(WIN)
    table = jnp.where(inside[:, None, :], table, 0.0)
    return table.astype(jnp.bfloat16)


def local_spectra(extended, sample_offsets, dft_rows):
    count_of_shots = sample_offsets.shape[0]
    reach_blocks = WIN // SPACING + 1
    jitter = sample_offsets - jnp.arange(count_of_shots, dtype=jnp.int32) * SPACING
    tables = shifted_tables(jitter, reach_blocks * SPACING)
    tables = tables.reshape(count_of_shots, dft_rows.shape[1], reach_blocks, SPACING)
    blocks = extended.reshape(extended.shape[0], extended.shape[1] // SPACING, SPACING)
    total = jnp.zeros((count_of_shots, dft_rows.shape[1], extended.shape[0]), jnp.float32)
    for offset in range(reach_blocks):
        record_part = blocks[:, offset : offset + count_of_shots, :]
        total = total + jnp.einsum(
            "rsu,scu->scr", record_part, tables[:, :, offset, :], preferred_element_type=jnp.float32
        )
    return total


def gram_terms(left, right):
    nfreq = len(freq_bins)
    left_re = left[:, :nfreq, :]
    left_im = left[:, nfreq:, :]
    right_re = right[:, :nfreq, :]
    right_im = right[:, nfreq:, :]
    gram_real = jnp.einsum("sfr,sfq->frq", left_re, right_re, preferred_element_type=jnp.float32)
    gram_real = gram_real + jnp.einsum(
        "sfr,sfq->frq", left_im, right_im, preferred_element_type=jnp.float32
    )
    gram_imag = jnp.einsum("sfr,sfq->frq", left_re, right_im, preferred_element_type=jnp.float32)
    gram_imag = gram_imag - jnp.einsum(
        "sfr,sfq->frq", left_im, right_re, preferred_element_type=jnp.float32
    )
    return jnp.stack([gram_real, gram_imag], axis=0)


def per_device(record, shot_fire_samples):
    trace_segment_length = record.shape[1]
    count_of_shots = shot_fire_samples.shape[0]
    dft_rows = dft_table(WIN)
    sample_offsets = shot_fire_samples - lax.axis_index("shot") * trace_segment_length
    head_rows = record[:, :WIN]
    rim_rows = shifted(head_rows, "shot", -1)
    extended = jnp.concatenate([record, rim_rows], axis=1)
    trace_spectra = local_spectra(extended, sample_offsets, dft_rows)
    trace_spectra = trace_spectra.astype(jnp.bfloat16)
    all_receivers = lax.all_gather(trace_spectra, "rcv", axis=2, tiled=True)
    total_shots = count_of_shots * lax.axis_size("shot")
    row_side = lax.all_gather(trace_spectra, "shot", axis=0, tiled=True)
    column_side = lax.all_to_all(all_receivers, "shot", split_axis=2, concat_axis=0, tiled=True)
    result = gram_terms(row_side, column_side)
    return result / total_shots


LANES = 128
HALF = 16
GROUP = 8
MESH = pl.DeviceIdType.MESH


def lane_fields(shape):
    lane = lax.broadcasted_iota(jnp.int32, shape, len(shape) - 1)
    return lane // 32 % 4, lane // 16 % 2, lane % 16


def rotated(lag):
    freq, part, _ = lane_fields((1, LANES))
    bins = jnp.full((1, LANES), freq_bins[0], jnp.int32)
    for f in range(1, len(freq_bins)):
        bins = jnp.where(freq == f, freq_bins[f], bins)
    turn = (lag & (SPACING - 1)) * bins + part * (WIN // 4)
    turn = ((turn + WIN // 2) & (WIN - 1)) - WIN // 2
    x = (math.pi / WIN) * turn.astype(jnp.float32)
    y = x * x
    series = 1.0 / math.factorial(13)
    for k in (11, 9, 7, 5, 3, 1):
        series = series * y + (-1.0) ** (k // 2) / math.factorial(k)
    half_sine = x * series
    return (1.0 - 2.0 * half_sine * half_sine) / math.sqrt(WIN)


def kernel(
    n, fire_hbm, rec_ref, out_ref,
    fire_ref, fire_sem, rec, joff, poff, table, tmask, rim_out, rim_in, gat, col, rmat, acc,
    rec_sem, jit_sem, rim_sem, ring_send, pair_send, chunk_recv, col_send, col_recv,
):
    me = lax.axis_index("shot")
    mj = lax.axis_index("rcv")
    rows = rec.shape[0]
    span = GROUP * SPACING
    chips = n // 2
    nz = chips // 2
    ncol = col.shape[2]
    shift, reach = SPACING.bit_length() - 1, WIN // SPACING
    core = me % 2
    chip = me // 2
    z, y = chip // 2, chip % 2
    pos = jnp.where(y == 0, z, chips - 1 - z)

    def device_at(position, which):
        q = (position + 2 * chips) % chips
        second = q >= nz
        zz = jnp.where(second, chips - 1 - q, q)
        yy = jnp.where(second, 1, 0)
        return (zz * 2 + yy) * 2 + which

    cw, ccw = device_at(pos + 1, core), device_at(pos - 1, core)
    pair = chip * 2 + (1 - core)
    prev, nxt = (me + n - 1) % n, (me + 1) % n

    def load(g):
        part = pl.ds(g * span, span)
        return pltpu.make_async_copy(rec_ref.at[:, part], rec.at[:, part], rec_sem.at[g])

    fires = pltpu.make_async_copy(fire_hbm, fire_ref, fire_sem)
    fires.start()
    for g in (1, 2, 0, 3):
        load(g).start()

    barrier = pltpu.get_barrier_semaphore()
    for other in (cw, ccw, pair, prev, nxt):
        pl.semaphore_signal(barrier, inc=1, device_id=(other, mj), device_id_type=MESH)
    pl.semaphore_signal(barrier, inc=1, device_id=(me, 1 - mj), device_id_type=MESH)
    fires.wait()
    _, _, shot_lane = lane_fields((1, LANES))
    offs = []
    for h in range(2):
        row = jnp.zeros((1, LANES), jnp.int32)
        for s in range(HALF):
            row = jnp.where(shot_lane == s, fire_ref[h * HALF + s], row)
        offs.append(row - me * rec.shape[1])
    joff[...] = jnp.broadcast_to(offs[1], joff.shape)

    jitter = pltpu.make_async_remote_copy(
        joff, poff, jit_sem.at[0], jit_sem.at[1], device_id=(nxt, mj), device_id_type=MESH
    )

    def fill_tables(kind, off_row):
        u = lax.broadcasted_iota(jnp.int32, (SPACING, LANES), 0)
        start = off_row & (SPACING - 1)
        value = rotated(u - start)
        table[kind, 0] = jnp.where(u >= start, value, 0.0).astype(jnp.bfloat16)
        table[kind, 1] = jnp.where(u < start, value, 0.0).astype(jnp.bfloat16)

    def group_dot(g, kinds):
        for slot, (kind, off_row) in enumerate(kinds):
            block_of = jnp.broadcast_to(off_row >> shift, (16, LANES))
            lanes = slice(slot * LANES, (slot + 1) * LANES)
            for b in range(GROUP):
                order = g * GROUP + b - block_of
                early = ((order >= 0) & (order < reach)).astype(jnp.float32).astype(jnp.bfloat16)
                late = ((order >= 1) & (order <= reach)).astype(jnp.float32).astype(jnp.bfloat16)
                block = (SPACING // 16, 16, LANES)
                mixed = table[kind, 0].reshape(block) * early + table[kind, 1].reshape(block) * late
                tmask[b * SPACING : (b + 1) * SPACING, lanes] = mixed.reshape(SPACING, LANES)
        return jnp.dot(
            rec[:, g * span : (g + 1) * span], tmask[:, : len(kinds) * LANES],
            preferred_element_type=jnp.float32,
        )

    def ring(src, h, d):
        return pltpu.make_async_remote_copy(
            gat.at[src, h], gat.at[src, h], ring_send.at[d, src, h], chunk_recv.at[src, h],
            device_id=(cw if d == 0 else ccw, mj), device_id_type=MESH,
        )

    def share(src, h):
        return pltpu.make_async_remote_copy(
            gat.at[src, h], gat.at[src, h], pair_send.at[src, h], chunk_recv.at[src, h],
            device_id=(pair, mj), device_id_type=MESH,
        )

    home = me * ncol // rows
    provider = home == mj
    first = pl.multiple_of(jnp.where(provider, me * ncol - home * rows, 0), 16)

    def col_far(src, h):
        return pltpu.make_async_remote_copy(
            gat.at[src, h, pl.ds(first, ncol), :], col.at[src, h], col_send.at[src, h],
            col_recv.at[src, h], device_id=(me, 1 - mj), device_id_type=MESH,
        )

    def col_near(src, h):
        return pltpu.make_async_copy(
            gat.at[src, h, pl.ds(first, ncol), :], col.at[src, h], col_recv.at[src, h]
        )

    def send_col(src, h):
        @pl.when(provider)
        def _():
            col_far(src, h).start()
            col_near(src, h).start()

    def send_own(h):
        ring(me, h, 0).start()
        ring(me, h, 1).start()
        share(me, h).start()
        send_col(me, h)

    def gram(src):
        for h in range(2):
            x = col[src, h].astype(jnp.float32)
            freq, part, _ = lane_fields(x.shape)
            swapped = jnp.where(part == 0, pltpu.roll(x, LANES - 16, 1), -pltpu.roll(x, 16, 1))
            for ri, value in enumerate((x, swapped)):
                for f in range(4):
                    rmat[pl.ds((ri * 4 + f) * ncol, ncol), h * LANES : (h + 1) * LANES] = jnp.where(
                        freq == f, value, 0.0
                    ).astype(jnp.bfloat16)
        left = jnp.concatenate([gat[src, 0], gat[src, 1]], axis=1)
        acc[...] += lax.dot_general(
            rmat[...], left, (((1,), (1,)), ((), ())), preferred_element_type=jnp.float32
        )

    half = chips // 2

    def hops(h, d):
        return half if h == d else half - 1

    def arrivals(t):
        found = []
        for h in range(2):
            for d in range(2):
                if 1 <= t <= hops(h, d):
                    found.append((h, d))
        return found

    def source(t, d, which):
        return device_at(pos - t if d == 0 else pos + t, which)

    def step_sources(t):
        if t == 0:
            return [0]
        return [0, 1] if t < half else [0]

    def gram_step(t):
        for which in (core, 1 - core):
            for d in step_sources(t):
                src = source(t, d, which)
                for h in range(2):
                    col_near(src, h).wait()
                gram(src)

    def ring_stage(h, t):
        for hh, d in arrivals(t):
            if hh == h:
                src = source(t, d, core)
                ring(src, h, d).wait_recv()
                if t < hops(h, d):
                    ring(src, h, d).start()
                share(src, h).start()
                send_col(src, h)

    def pair_stage(h, t):
        ways = [0] if t == 0 else [d for hh, d in arrivals(t) if hh == h]
        for d in ways:
            src = source(t, d, 1 - core)
            share(src, h).wait_recv()
            send_col(src, h)

    fill_tables(0, offs[0])
    fill_tables(1, offs[1])
    acc[...] = jnp.zeros_like(acc)
    kinds = ((0, offs[0]), (1, offs[1]))
    load(1).wait()
    own = group_dot(1, kinds[:1])
    pl.semaphore_wait(barrier, 6)
    jitter.start()
    load(2).wait()
    both = group_dot(2, kinds)
    load(0).wait()
    own = own + both[:, :LANES] + group_dot(0, kinds[:1])
    gat[me, 0] = own.astype(jnp.bfloat16)
    send_own(0)
    jitter.wait()
    offp = poff[0:1, :] - rec.shape[1]
    fill_tables(2, offp)
    foreign = group_dot(0, ((2, offp),))
    cut = rows // 2
    rim_out[...] = foreign[:cut] + pltpu.roll(foreign[cut:], LANES - 8, 1)
    rim = pltpu.make_async_remote_copy(
        rim_out, rim_in, rim_sem.at[0], rim_sem.at[1], device_id=(prev, mj), device_id_type=MESH
    )
    rim.start()
    load(3).wait()
    second = both[:, LANES:] + group_dot(3, kinds[1:])
    ring_stage(0, 1)
    rim.wait()
    _, _, shot = lane_fields((cut, LANES))
    wanted = (shot >= 8) & (me < n - 1)
    upper = jnp.where(wanted, rim_in[...], 0.0)
    lower = jnp.where(wanted, pltpu.roll(rim_in[...], 8, 1), 0.0)
    gat[me, 1, :cut] = (second[:cut] + upper).astype(jnp.bfloat16)
    gat[me, 1, cut:] = (second[cut:] + lower).astype(jnp.bfloat16)
    send_own(1)

    pair_stage(0, 0)
    for t in range(1, half + 1):
        ring_stage(0, t + 1)
        ring_stage(1, t)
        pair_stage(0, t)
        pair_stage(1, t - 1)
        gram_step(t - 1)
    pair_stage(1, half)
    gram_step(half)

    scale = 1.0 / (n * 2 * HALF)
    for g in range(8):
        out_ref[g // 4, g % 4] = acc[g * ncol : (g + 1) * ncol, :] * scale

    for h in range(2):
        ring(me, h, 0).wait_send()
        ring(me, h, 1).wait_send()
    for t in range(1, half + 1):
        for h, d in arrivals(t):
            src = source(t, d, core)
            if t < hops(h, d):
                ring(src, h, d).wait_send()
            share(src, h).wait_send()
    for h in range(2):
        share(me, h).wait_send()

    @pl.when(provider)
    def _():
        for src in range(n):
            for h in range(2):
                col_far(src, h).wait_send()


def fused_device(n, ncol, record, shot_fire_samples):
    rows, length = record.shape
    gram = pl.pallas_call(
        functools.partial(kernel, n),
        out_shape=jax.ShapeDtypeStruct((2, 4, ncol, rows), jnp.float32),
        in_specs=[
            pl.BlockSpec(memory_space=pltpu.HBM),
            pl.BlockSpec(memory_space=pltpu.HBM),
        ],
        out_specs=pl.BlockSpec(memory_space=pltpu.VMEM),
        scratch_shapes=[
            pltpu.SMEM(shot_fire_samples.shape, jnp.int32),
            pltpu.SemaphoreType.DMA,
            pltpu.VMEM((rows, length), jnp.bfloat16),
            pltpu.VMEM((8, LANES), jnp.int32),
            pltpu.VMEM((8, LANES), jnp.int32),
            pltpu.VMEM((3, 2, SPACING, LANES), jnp.bfloat16),
            pltpu.VMEM((GROUP * SPACING, 2 * LANES), jnp.bfloat16),
            pltpu.VMEM((rows // 2, LANES), jnp.float32),
            pltpu.VMEM((rows // 2, LANES), jnp.float32),
            pltpu.VMEM((n, 2, rows, LANES), jnp.bfloat16),
            pltpu.VMEM((n, 2, ncol, LANES), jnp.bfloat16),
            pltpu.VMEM((8 * ncol, 2 * LANES), jnp.bfloat16),
            pltpu.VMEM((8 * ncol, rows), jnp.float32),
            pltpu.SemaphoreType.DMA((length // (GROUP * SPACING),)),
            pltpu.SemaphoreType.DMA((2,)),
            pltpu.SemaphoreType.DMA((2,)),
            pltpu.SemaphoreType.DMA((2, n, 2)),
            pltpu.SemaphoreType.DMA((n, 2)),
            pltpu.SemaphoreType.DMA((n, 2)),
            pltpu.SemaphoreType.DMA((n, 2)),
            pltpu.SemaphoreType.DMA((n, 2)),
        ],
        compiler_params=pltpu.CompilerParams(
            collective_id=0, has_side_effects=True, vmem_limit_bytes=50 * 1024 * 1024
        ),
    )(shot_fire_samples, record)
    return gram.transpose(0, 1, 3, 2)


def whole_step(n, receivers, record, shot_fire_samples):
    rows, length = record.shape
    shots = shot_fire_samples.shape[0]
    ncol = receivers // n
    fits = (
        receivers == 2 * rows and ncol % 16 == 0 and rows % (2 * ncol) == 0
        and shots == 2 * HALF and length == shots * SPACING and n % 8 == 0
    )
    if fits:
        return fused_device(n, ncol, record, shot_fire_samples)
    return per_device(record, shot_fire_samples)


def solution(mesh):
    def step(record, shot_fire_samples):
        body = functools.partial(whole_step, mesh.shape["shot"], record.shape[0])
        return jax.shard_map(
            body,
            mesh=mesh,
            in_specs=(P("rcv", "shot"), P("shot")),
            out_specs=P(None, None, "rcv", "shot"),
            check_vma=False,
        )(record, shot_fire_samples)

    return step
```

```python
import functools
import math

import jax
import jax.numpy as jnp
from jax import lax
from jax.experimental import pallas as pl
from jax.experimental.pallas import tpu as pltpu
from jax.sharding import PartitionSpec as P

WIN = 2048
SPACING = 256


freq_bins = (24, 40, 56, 80)


def shifted(block, axis, distance):
    devices = range(lax.axis_size(axis))
    route = [(i - distance, i) for i in devices if i - distance in devices]
    return lax.ppermute(block, axis, route)


def dft_table(window_len):
    lag_index = jnp.arange(window_len, dtype=jnp.int32)
    bin_list = jnp.array(freq_bins, dtype=jnp.int32)
    turn_count = lag_index[:, None] * bin_list[None, :] % window_len
    phase_angle = 2.0 * math.pi / window_len * turn_count.astype(jnp.float32)
    dft_rows = jnp.concatenate([jnp.cos(phase_angle), -jnp.sin(phase_angle)], axis=1) / math.sqrt(
        window_len
    )
    return dft_rows.astype(jnp.bfloat16)


def shifted_tables(jitter, span):
    lag_index = jnp.arange(span, dtype=jnp.int32)[None, :] - jitter[:, None]
    inside = (lag_index >= 0) & (lag_index < WIN)
    clipped = jnp.clip(lag_index, 0, WIN - 1)
    bin_list = jnp.array(freq_bins, dtype=jnp.int32)
    turn_count = clipped[:, None, :] * bin_list[None, :, None] % WIN
    phase_angle = 2.0 * math.pi / WIN * turn_count.astype(jnp.float32)
    table = jnp.concatenate([jnp.cos(phase_angle), -jnp.sin(phase_angle)], axis=1) / math.sqrt(WIN)
    table = jnp.where(inside[:, None, :], table, 0.0)
    return table.astype(jnp.bfloat16)


def local_spectra(extended, sample_offsets, dft_rows):
    count_of_shots = sample_offsets.shape[0]
    reach_blocks = WIN // SPACING + 1
    jitter = sample_offsets - jnp.arange(count_of_shots, dtype=jnp.int32) * SPACING
    tables = shifted_tables(jitter, reach_blocks * SPACING)
    tables = tables.reshape(count_of_shots, dft_rows.shape[1], reach_blocks, SPACING)
    blocks = extended.reshape(extended.shape[0], extended.shape[1] // SPACING, SPACING)
    total = jnp.zeros((count_of_shots, dft_rows.shape[1], extended.shape[0]), jnp.float32)
    for offset in range(reach_blocks):
        record_part = blocks[:, offset : offset + count_of_shots, :]
        total = total + jnp.einsum(
            "rsu,scu->scr", record_part, tables[:, :, offset, :], preferred_element_type=jnp.float32
        )
    return total


def gram_terms(left, right):
    nfreq = len(freq_bins)
    left_re = left[:, :nfreq, :]
    left_im = left[:, nfreq:, :]
    right_re = right[:, :nfreq, :]
    right_im = right[:, nfreq:, :]
    gram_real = jnp.einsum("sfr,sfq->frq", left_re, right_re, preferred_element_type=jnp.float32)
    gram_real = gram_real + jnp.einsum(
        "sfr,sfq->frq", left_im, right_im, preferred_element_type=jnp.float32
    )
    gram_imag = jnp.einsum("sfr,sfq->frq", left_re, right_im, preferred_element_type=jnp.float32)
    gram_imag = gram_imag - jnp.einsum(
        "sfr,sfq->frq", left_im, right_re, preferred_element_type=jnp.float32
    )
    return jnp.stack([gram_real, gram_imag], axis=0)


def per_device(record, shot_fire_samples):
    trace_segment_length = record.shape[1]
    count_of_shots = shot_fire_samples.shape[0]
    dft_rows = dft_table(WIN)
    sample_offsets = shot_fire_samples - lax.axis_index("shot") * trace_segment_length
    head_rows = record[:, :WIN]
    rim_rows = shifted(head_rows, "shot", -1)
    extended = jnp.concatenate([record, rim_rows], axis=1)
    trace_spectra = local_spectra(extended, sample_offsets, dft_rows)
    trace_spectra = trace_spectra.astype(jnp.bfloat16)
    all_receivers = lax.all_gather(trace_spectra, "rcv", axis=2, tiled=True)
    total_shots = count_of_shots * lax.axis_size("shot")
    row_side = lax.all_gather(trace_spectra, "shot", axis=0, tiled=True)
    column_side = lax.all_to_all(all_receivers, "shot", split_axis=2, concat_axis=0, tiled=True)
    result = gram_terms(row_side, column_side)
    return result / total_shots


LANES = 128
HALF = 16
GROUP = 8
MESH = pl.DeviceIdType.MESH


def lane_fields(shape):
    lane = lax.broadcasted_iota(jnp.int32, shape, len(shape) - 1)
    return lane // 32 % 4, lane // 16 % 2, lane % 16


def rotated(lag):
    freq, part, _ = lane_fields((1, LANES))
    bins = jnp.full((1, LANES), freq_bins[0], jnp.int32)
    for f in range(1, len(freq_bins)):
        bins = jnp.where(freq == f, freq_bins[f], bins)
    turn = (lag & (SPACING - 1)) * bins + part * (WIN // 4)
    turn = ((turn + WIN // 2) & (WIN - 1)) - WIN // 2
    x = (math.pi / WIN) * turn.astype(jnp.float32)
    y = x * x
    series = 1.0 / math.factorial(13)
    for k in (11, 9, 7, 5, 3, 1):
        series = series * y + (-1.0) ** (k // 2) / math.factorial(k)
    half_sine = x * series
    return (1.0 - 2.0 * half_sine * half_sine) / math.sqrt(WIN)


def kernel(
    n, fire_hbm, rec_ref, out_ref,
    fire_ref, fire_sem, rec, joff, poff, table, tmask, rim_out, rim_in, gat, col, rmat, acc,
    rec_sem, jit_sem, rim_sem, ring_send, pair_send, chunk_recv, col_send, col_recv,
):
    me = lax.axis_index("shot")
    mj = lax.axis_index("rcv")
    rows = rec.shape[0]
    span = GROUP * SPACING
    chips = n // 2
    nz = chips // 2
    ncol = col.shape[2]
    shift, reach = SPACING.bit_length() - 1, WIN // SPACING
    core = me % 2
    chip = me // 2
    z, y = chip // 2, chip % 2
    pos = jnp.where(y == 0, z, chips - 1 - z)

    def device_at(position, which):
        q = (position + 2 * chips) % chips
        second = q >= nz
        zz = jnp.where(second, chips - 1 - q, q)
        yy = jnp.where(second, 1, 0)
        return (zz * 2 + yy) * 2 + which

    cw, ccw = device_at(pos + 1, core), device_at(pos - 1, core)
    pair = chip * 2 + (1 - core)
    prev, nxt = (me + n - 1) % n, (me + 1) % n

    def load(g):
        part = pl.ds(g * span, span)
        return pltpu.make_async_copy(rec_ref.at[:, part], rec.at[:, part], rec_sem.at[g])

    fires = pltpu.make_async_copy(fire_hbm, fire_ref, fire_sem)
    fires.start()
    for g in (1, 2, 0, 3):
        load(g).start()

    barrier = pltpu.get_barrier_semaphore()
    for other in (cw, ccw, pair, prev, nxt):
        pl.semaphore_signal(barrier, inc=1, device_id=(other, mj), device_id_type=MESH)
    pl.semaphore_signal(barrier, inc=1, device_id=(me, 1 - mj), device_id_type=MESH)
    fires.wait()
    _, _, shot_lane = lane_fields((1, LANES))
    offs = []
    for h in range(2):
        row = jnp.zeros((1, LANES), jnp.int32)
        for s in range(HALF):
            row = jnp.where(shot_lane == s, fire_ref[h * HALF + s], row)
        offs.append(row - me * rec.shape[1])
    joff[...] = jnp.broadcast_to(offs[1], joff.shape)

    jitter = pltpu.make_async_remote_copy(
        joff, poff, jit_sem.at[0], jit_sem.at[1], device_id=(nxt, mj), device_id_type=MESH
    )

    def fill_tables(kind, off_row):
        u = lax.broadcasted_iota(jnp.int32, (SPACING, LANES), 0)
        start = off_row & (SPACING - 1)
        value = rotated(u - start)
        table[kind, 0] = jnp.where(u >= start, value, 0.0).astype(jnp.bfloat16)
        table[kind, 1] = jnp.where(u < start, value, 0.0).astype(jnp.bfloat16)

    def group_dot(g, kinds):
        for slot, (kind, off_row) in enumerate(kinds):
            block_of = jnp.broadcast_to(off_row >> shift, (16, LANES))
            lanes = slice(slot * LANES, (slot + 1) * LANES)
            for b in range(GROUP):
                order = g * GROUP + b - block_of
                early = ((order >= 0) & (order < reach)).astype(jnp.float32).astype(jnp.bfloat16)
                late = ((order >= 1) & (order <= reach)).astype(jnp.float32).astype(jnp.bfloat16)
                block = (SPACING // 16, 16, LANES)
                mixed = table[kind, 0].reshape(block) * early + table[kind, 1].reshape(block) * late
                tmask[b * SPACING : (b + 1) * SPACING, lanes] = mixed.reshape(SPACING, LANES)
        return jnp.dot(
            rec[:, g * span : (g + 1) * span], tmask[:, : len(kinds) * LANES],
            preferred_element_type=jnp.float32,
        )

    def ring(src, h, d):
        return pltpu.make_async_remote_copy(
            gat.at[src, h], gat.at[src, h], ring_send.at[d, src, h], chunk_recv.at[src, h],
            device_id=(cw if d == 0 else ccw, mj), device_id_type=MESH,
        )

    def share(src, h):
        return pltpu.make_async_remote_copy(
            gat.at[src, h], gat.at[src, h], pair_send.at[src, h], chunk_recv.at[src, h],
            device_id=(pair, mj), device_id_type=MESH,
        )

    home = me * ncol // rows
    provider = home == mj
    first = pl.multiple_of(jnp.where(provider, me * ncol - home * rows, 0), 16)

    def col_far(src, h):
        return pltpu.make_async_remote_copy(
            gat.at[src, h, pl.ds(first, ncol), :], col.at[src, h], col_send.at[src, h],
            col_recv.at[src, h], device_id=(me, 1 - mj), device_id_type=MESH,
        )

    def col_near(src, h):
        return pltpu.make_async_copy(
            gat.at[src, h, pl.ds(first, ncol), :], col.at[src, h], col_recv.at[src, h]
        )

    def send_col(src, h):
        @pl.when(provider)
        def _():
            col_far(src, h).start()
            col_near(src, h).start()

    def send_own(h):
        ring(me, h, h).start()
        ring(me, h, 1 - h).start()
        share(me, h).start()
        send_col(me, h)

    def gram(src):
        for h in range(2):
            x = col[src, h].astype(jnp.float32)
            freq, part, _ = lane_fields(x.shape)
            swapped = jnp.where(part == 0, pltpu.roll(x, LANES - 16, 1), -pltpu.roll(x, 16, 1))
            for ri, value in enumerate((x, swapped)):
                for f in range(4):
                    rmat[pl.ds((ri * 4 + f) * ncol, ncol), h * LANES : (h + 1) * LANES] = jnp.where(
                        freq == f, value, 0.0
                    ).astype(jnp.bfloat16)
        left = jnp.concatenate([gat[src, 0], gat[src, 1]], axis=1)
        acc[...] += lax.dot_general(
            rmat[...], left, (((1,), (1,)), ((), ())), preferred_element_type=jnp.float32
        )

    fill_tables(0, offs[0])
    fill_tables(1, offs[1])
    acc[...] = jnp.zeros_like(acc)
    kinds = ((0, offs[0]), (1, offs[1]))
    load(1).wait()
    own = group_dot(1, kinds[:1])
    pl.semaphore_wait(barrier, 6)
    jitter.start()
    load(2).wait()
    both = group_dot(2, kinds)
    load(0).wait()
    own = own + both[:, :LANES] + group_dot(0, kinds[:1])
    gat[me, 0] = own.astype(jnp.bfloat16)
    send_own(0)
    jitter.wait()
    offp = poff[0:1, :] - rec.shape[1]
    fill_tables(2, offp)
    foreign = group_dot(0, ((2, offp),))
    cut = rows // 2
    rim_out[...] = foreign[:cut] + pltpu.roll(foreign[cut:], LANES - 8, 1)
    rim = pltpu.make_async_remote_copy(
        rim_out, rim_in, rim_sem.at[0], rim_sem.at[1], device_id=(prev, mj), device_id_type=MESH
    )
    rim.start()
    load(3).wait()
    second = both[:, LANES:] + group_dot(3, kinds[1:])
    rim.wait()
    _, _, shot = lane_fields((cut, LANES))
    wanted = (shot >= 8) & (me < n - 1)
    upper = jnp.where(wanted, rim_in[...], 0.0)
    lower = jnp.where(wanted, pltpu.roll(rim_in[...], 8, 1), 0.0)
    gat[me, 1, :cut] = (second[:cut] + upper).astype(jnp.bfloat16)
    gat[me, 1, cut:] = (second[cut:] + lower).astype(jnp.bfloat16)
    send_own(1)

    half = chips // 2

    def hops(h, d):
        return half if h == d else half - 1

    def arrivals(t):
        found = []
        for h in range(2):
            for d in range(2):
                if 1 <= t <= hops(h, d):
                    found.append((h, d))
        return found

    def source(t, d, which):
        return device_at(pos - t if d == 0 else pos + t, which)

    def step_sources(t):
        if t == 0:
            return [0]
        return [0, 1] if t < half else [0]

    def gram_step(t):
        for which in (core, 1 - core):
            for d in step_sources(t):
                src = source(t, d, which)
                for h in range(2):
                    col_near(src, h).wait()
                gram(src)

    for t in range(half + 1):
        for h, d in arrivals(t):
            src = source(t, d, core)
            ring(src, h, d).wait_recv()
            if t < hops(h, d):
                ring(src, h, d).start()
            share(src, h).start()
            send_col(src, h)
        if t > 0:
            gram_step(t - 1)
        for d in step_sources(t):
            for h in range(2):
                src = source(t, d, 1 - core)
                share(src, h).wait_recv()
                send_col(src, h)
    gram_step(half)

    scale = 1.0 / (n * 2 * HALF)
    for g in range(8):
        out_ref[g // 4, g % 4] = acc[g * ncol : (g + 1) * ncol, :] * scale

    for h in range(2):
        ring(me, h, 0).wait_send()
        ring(me, h, 1).wait_send()
    for t in range(1, half + 1):
        for h, d in arrivals(t):
            src = source(t, d, core)
            if t < hops(h, d):
                ring(src, h, d).wait_send()
            share(src, h).wait_send()
    for h in range(2):
        share(me, h).wait_send()

    @pl.when(provider)
    def _():
        for src in range(n):
            for h in range(2):
                col_far(src, h).wait_send()


def fused_device(n, ncol, record, shot_fire_samples):
    rows, length = record.shape
    gram = pl.pallas_call(
        functools.partial(kernel, n),
        out_shape=jax.ShapeDtypeStruct((2, 4, ncol, rows), jnp.float32),
        in_specs=[
            pl.BlockSpec(memory_space=pltpu.HBM),
            pl.BlockSpec(memory_space=pltpu.HBM),
        ],
        out_specs=pl.BlockSpec(memory_space=pltpu.VMEM),
        scratch_shapes=[
            pltpu.SMEM(shot_fire_samples.shape, jnp.int32),
            pltpu.SemaphoreType.DMA,
            pltpu.VMEM((rows, length), jnp.bfloat16),
            pltpu.VMEM((8, LANES), jnp.int32),
            pltpu.VMEM((8, LANES), jnp.int32),
            pltpu.VMEM((3, 2, SPACING, LANES), jnp.bfloat16),
            pltpu.VMEM((GROUP * SPACING, 2 * LANES), jnp.bfloat16),
            pltpu.VMEM((rows // 2, LANES), jnp.float32),
            pltpu.VMEM((rows // 2, LANES), jnp.float32),
            pltpu.VMEM((n, 2, rows, LANES), jnp.bfloat16),
            pltpu.VMEM((n, 2, ncol, LANES), jnp.bfloat16),
            pltpu.VMEM((8 * ncol, 2 * LANES), jnp.bfloat16),
            pltpu.VMEM((8 * ncol, rows), jnp.float32),
            pltpu.SemaphoreType.DMA((length // (GROUP * SPACING),)),
            pltpu.SemaphoreType.DMA((2,)),
            pltpu.SemaphoreType.DMA((2,)),
            pltpu.SemaphoreType.DMA((2, n, 2)),
            pltpu.SemaphoreType.DMA((n, 2)),
            pltpu.SemaphoreType.DMA((n, 2)),
            pltpu.SemaphoreType.DMA((n, 2)),
            pltpu.SemaphoreType.DMA((n, 2)),
        ],
        compiler_params=pltpu.CompilerParams(
            collective_id=0, has_side_effects=True, vmem_limit_bytes=50 * 1024 * 1024
        ),
    )(shot_fire_samples, record)
    return gram.transpose(0, 1, 3, 2)


def whole_step(n, receivers, record, shot_fire_samples):
    rows, length = record.shape
    shots = shot_fire_samples.shape[0]
    ncol = receivers // n
    fits = (
        receivers == 2 * rows and ncol % 16 == 0 and rows % (2 * ncol) == 0
        and shots == 2 * HALF and length == shots * SPACING and n % 8 == 0
    )
    if fits:
        return fused_device(n, ncol, record, shot_fire_samples)
    return per_device(record, shot_fire_samples)


def solution(mesh):
    def step(record, shot_fire_samples):
        body = functools.partial(whole_step, mesh.shape["shot"], record.shape[0])
        return jax.shard_map(
            body,
            mesh=mesh,
            in_specs=(P("rcv", "shot"), P("shot")),
            out_specs=P(None, None, "rcv", "shot"),
            check_vma=False,
        )(record, shot_fire_samples)

    return step
```
